32 devices in a mesh: fsdp: 8 (over y, x, core), rep: 4 (over z).
Axes of the slice: x: 2, y: 2, z: 4, core: 2. Of those that a mesh axis runs over, the one named last changes fastest.
Arguments:
- layer_input: bfloat16 [128, 512, 768], P(('fsdp', 'rep')), may hold values from -6 to 6
- segment_length_pairs: int32 [128, 2], P(('fsdp', 'rep')), may hold values from 16 to 496, as said below
- query_key_value_weight: bfloat16 [3, 768, 768], P(None, 'fsdp', 'rep'), may hold values from -0.21875 to 0.21875
- output_weight: bfloat16 [768, 768], P('fsdp', 'rep'), may hold values from -0.875 to 0.875
- attention_bias: bfloat16 [3, 768], P(None, 'fsdp'), may hold values from -1.5 to 1.5
- adapter_down: bfloat16 [2, 768, 8], P(None, 'fsdp'), may hold values from -0.21875 to 0.21875
- adapter_up: bfloat16 [2, 8, 768], replicated, may hold values from -1 to 1
- layernorm_gain: bfloat16 [2, 768], P(None, 'fsdp'), may hold values from 0.5 to 1.5
- layernorm_bias: bfloat16 [2, 768], P(None, 'fsdp'), may hold values from -1.5 to 1.5
- feedforward_in_weight: bfloat16 [768, 3072], P('fsdp', 'rep'), may hold values from -0.21875 to 0.21875
- feedforward_in_bias: bfloat16 [3072], P('fsdp'), may hold values from -1.5 to 1.5
- feedforward_out_weight: bfloat16 [3072, 768], P('fsdp', 'rep'), may hold values from -0.21875 to 0.21875
- feedforward_out_bias: bfloat16 [768], P('fsdp'), may hold values from -1.5 to 1.5
- output_cotangent: bfloat16 [128, 512, 768], P(('fsdp', 'rep')), may hold values from -6 to 6
Outputs:
- hidden_out: bfloat16 [128, 512, 768], P(('fsdp', 'rep'))
- hidden_grad: bfloat16 [128, 512, 768], P(('fsdp', 'rep'))
- adapter_up_gradient: float32 [2, 8, 768], replicated
The draws below stay inside these ranges and needn't reach their ends.
Inputs may be any that keep to these rules, and one draw needn't show every extreme that they name: Item i uses slots 0 to segment_length_pairs[i,0] + segment_length_pairs[i,1] - 1 of its 512; that total is at most 512, and exactly 512 for every item whose index is a multiple of 4. The first segment is at most 256. Item 0 has a first segment of 16 and a second of 496; item 1 has a second segment of 16.
All inputs are finite; a program needn't handle non-finite values.
Results may differ from the reference program's by a relative error of at most 0.017.
Values may be sent and summed in bfloat16 or wider, within the bound.
No kernel may reach another device: no remote copies, remote signals or barrier semaphores. Data moves between devices by JAX's collectives and lax.ppermute only.
A program may use at most 320 MiB of HBM per device.

```python
import math
import jax
import jax.numpy as jnp
from jax import lax

MODEL_WIDTH = 768
H = 12
HD = 64
FF = 3072
ADAPTER_RANK = 8
ADAPTER_ALPHA = 16
L = 512
ITEMS_DEV = 4
ITEMS = 128
TOKENS = 65536


def draw_segment_length_pairs(key, part):
    first_key, second_key = jax.random.split(key)
    shortest = max(L // 32, 1)
    item_index = jnp.arange(ITEMS)
    first_len = jax.random.randint(first_key, (ITEMS,), shortest, L // 2 + 1)
    first_len = jnp.where(item_index == 0, shortest, first_len)
    raw_bits = jax.random.randint(second_key, (ITEMS,), 0, 1 << 20)
    spare_room = L - first_len - shortest + 1
    second_len = shortest + raw_bits % spare_room
    second_len = jnp.where(item_index == 1, shortest, second_len)
    full_item = item_index % ITEMS_DEV == 0
    second_len = jnp.where(full_item, L - first_len, second_len)
    return jnp.stack([first_len, second_len], axis=1).astype(jnp.int32)


def draw_output_cotangent(key, part):
    noise_key = jax.random.fold_in(key, 0)
    ramp_scale = 0.5 + jnp.arange(ITEMS, dtype=jnp.float32) / max(ITEMS - 1, 1)
    noise_draw = jnp.clip(jax.random.normal(noise_key, (ITEMS, L, MODEL_WIDTH), jnp.float32), -4.0, 4.0)
    return (ramp_scale[:, None, None] * noise_draw).astype(jnp.bfloat16)


def steps_of(key, shape, pieces, least, largest):
    loudness = 1.0
    for dim, blocks in pieces:
        steps = jax.random.uniform(jax.random.fold_in(jax.random.fold_in(key, 6), dim), (blocks,), jnp.float32, least / len(pieces), largest / len(pieces))
        loudness = loudness * jnp.repeat(jnp.exp(steps), shape[dim] // blocks).reshape((-1,) + (1,) * (len(shape) - 1 - dim))
    return loudness


def scatter_about(own_key, dims, width, reach, pieces=(), held_as=jnp.bfloat16):
    factor_of = steps_of(own_key, dims, pieces, -0.22, 0.18) if pieces else 1.0
    result = jax.random.normal(own_key, dims, jnp.float32) * width * factor_of
    return jnp.minimum(jnp.maximum(result, -reach), reach).astype(held_as)


def setup_inputs(seed: int = 0) -> dict:
    key_list = jax.random.split(jax.random.key(seed), 15)
    layer_input = scatter_about(key_list[0], (ITEMS, L, MODEL_WIDTH), 1.0, 6.0, ((0, 32),))
    segment_length_pairs = draw_segment_length_pairs(jax.random.fold_in(key_list[14], 71), 0)
    query_key_value_weight = scatter_about(key_list[2], (3, MODEL_WIDTH, MODEL_WIDTH), MODEL_WIDTH ** -0.5, 0.21875, ((1, 8), (2, 4)))
    output_weight = scatter_about(key_list[3], (MODEL_WIDTH, MODEL_WIDTH), (MODEL_WIDTH // 16) ** -0.5, 0.875, ((0, 8), (1, 4)))
    attention_bias = scatter_about(key_list[4], (3, MODEL_WIDTH), 0.3, 1.5, ((1, 8),))
    adapter_down = scatter_about(key_list[5], (2, MODEL_WIDTH, ADAPTER_RANK), MODEL_WIDTH ** -0.5, 0.21875, ((1, 8),))
    adapter_up = scatter_about(key_list[6], (2, ADAPTER_RANK, MODEL_WIDTH), 32 ** -0.5, 1.0)
    layernorm_gain = jnp.clip(1.0 + 0.1 * jax.random.normal(key_list[7], (2, MODEL_WIDTH), jnp.float32), 0.5, 1.5).astype(jnp.bfloat16)
    layernorm_bias = scatter_about(key_list[8], (2, MODEL_WIDTH), 0.3, 1.5, ((1, 8),))
    feedforward_in_weight = scatter_about(key_list[9], (MODEL_WIDTH, FF), MODEL_WIDTH ** -0.5, 0.21875, ((0, 8), (1, 4)))
    feedforward_in_bias = scatter_about(key_list[10], (FF,), 0.3, 1.5, ((0, 8),))
    feedforward_out_weight = scatter_about(key_list[11], (FF, MODEL_WIDTH), (FF // 4) ** -0.5, 0.21875, ((0, 8), (1, 4)))
    feedforward_out_bias = scatter_about(key_list[12], (MODEL_WIDTH,), 0.3, 1.5, ((0, 8),))
    output_cotangent = draw_output_cotangent(jax.random.fold_in(key_list[14], 71), 0)
    return dict(layer_input=layer_input, segment_length_pairs=segment_length_pairs, query_key_value_weight=query_key_value_weight, output_weight=output_weight, attention_bias=attention_bias, adapter_down=adapter_down, adapter_up=adapter_up, layernorm_gain=layernorm_gain, layernorm_bias=layernorm_bias, feedforward_in_weight=feedforward_in_weight, feedforward_in_bias=feedforward_in_bias, feedforward_out_weight=feedforward_out_weight, feedforward_out_bias=feedforward_out_bias, output_cotangent=output_cotangent)


@jax.custom_vjp
def reduced_precision(v):
    return lax.optimization_barrier(v.astype(jnp.bfloat16)).astype(jnp.float32)

@jax.custom_vjp
def reduced_reverse(v):
    return v

def low_keep(v):
    return (reduced_precision(v), None)

def low_pass(kept, grad):
    return (grad,)

def back_keep(v):
    return (v, None)

def back_low(kept, grad):
    return (reduced_precision(grad),)
reduced_precision.defvjp(low_keep, low_pass)
reduced_reverse.defvjp(back_keep, back_low)

def to_single_float(values):
    return values.astype(jnp.float32)

def norm_rows(values):
    centered = values - lax.optimization_barrier(jnp.mean(values, axis=-1, keepdims=True))
    spread = lax.optimization_barrier(jnp.mean(centered * centered, axis=-1, keepdims=True))
    return centered * lax.rsqrt(spread + 1e-05)

def layer_row_block(input_bundle, adapter_right, valid_counts, frozen_bundle):
    qkv_full, out_full, attention_offset, down_matrix_whole, norm_gains, norm_shifts, in_full, in_shift, back_full, back_shift = frozen_bundle
    highest_precision = lax.Precision.HIGHEST
    adapter_scale = ADAPTER_ALPHA / ADAPTER_RANK
    head_scale = 1.0 / math.sqrt(HD)
    batch_items = input_bundle.shape[0]
    adapter_left = reduced_precision(reduced_reverse(jnp.einsum('vim,bmz->vibz', input_bundle, down_matrix_whole, precision=highest_precision)))
    projected_rows = jnp.einsum('gld,kde->glke', input_bundle, qkv_full, precision=highest_precision)
    adapter_term = jnp.einsum('vezp,zpo->vezo', adapter_left, adapter_right, precision=highest_precision)
    query_rows = reduced_precision(reduced_reverse(projected_rows[:, :, 0] + attention_offset[0] + adapter_scale * adapter_term[:, :, 0]))
    key_vals = reduced_precision(reduced_reverse(projected_rows[:, :, 1]))
    value_rows = reduced_precision(reduced_reverse(projected_rows[:, :, 2] + attention_offset[1] + adapter_scale * adapter_term[:, :, 1]))
    head_shape = (batch_items, L, H, HD)
    scores = jnp.einsum('glhe,gmhe->ghlm', query_rows.reshape(head_shape), key_vals.reshape(head_shape), precision=highest_precision)
    scores = reduced_reverse(scores * head_scale)
    valid_keys = jnp.arange(L)[None, :] < valid_counts[:, None]
    scores = jnp.where(valid_keys[:, None, None, :], scores, -1e+30)
    attn_probs = reduced_precision(jax.nn.softmax(scores, axis=-1))
    mixed = jnp.einsum('ghlm,gmhe->glhe', attn_probs, value_rows.reshape(head_shape), precision=highest_precision)
    mixed = reduced_precision(reduced_reverse(mixed.reshape(batch_items, L, MODEL_WIDTH)))
    first_sum = input_bundle + reduced_reverse(jnp.einsum('gld,de->gle', mixed, out_full, precision=highest_precision)) + attention_offset[2]
    hidden_one = norm_rows(first_sum) * norm_gains[0] + norm_shifts[0]
    ffn_inner = reduced_reverse(jnp.einsum('gld,df->glf', reduced_precision(hidden_one), in_full, precision=highest_precision) + in_shift)
    activation = reduced_precision(jax.nn.gelu(ffn_inner, approximate=False))
    second_sum = hidden_one + reduced_reverse(jnp.einsum('glf,fd->gld', activation, back_full, precision=highest_precision)) + back_shift
    return norm_rows(second_sum) * norm_gains[1] + norm_shifts[1]

def reference(layer_input, segment_length_pairs, query_key_value_weight, output_weight, attention_bias, adapter_down, adapter_up, layernorm_gain, layernorm_bias, feedforward_in_weight, feedforward_in_bias, feedforward_out_weight, feedforward_out_bias, output_cotangent):
    frozen_bundle = (to_single_float(query_key_value_weight), to_single_float(output_weight), to_single_float(attention_bias), to_single_float(adapter_down), to_single_float(layernorm_gain), to_single_float(layernorm_bias), to_single_float(feedforward_in_weight), to_single_float(feedforward_in_bias), to_single_float(feedforward_out_weight), to_single_float(feedforward_out_bias))
    per_group = 8
    group_count = ITEMS // per_group
    live_all = (segment_length_pairs[:, 0] + segment_length_pairs[:, 1]).reshape(group_count, per_group)
    inputs_all = layer_input.reshape(group_count, per_group, L, MODEL_WIDTH)
    grads_all = output_cotangent.reshape(group_count, per_group, L, MODEL_WIDTH)
    adapter_right = to_single_float(adapter_up)

    def group_step(total_grad, batch):
        input_bundle, cotangent, valid_counts = batch

        def encoder_layer_apply(layer_in, right_in):
            return layer_row_block(layer_in, right_in, valid_counts, frozen_bundle)
        layer_output, reverse_function = jax.vjp(encoder_layer_apply, to_single_float(input_bundle), adapter_right)
        grad_in, grad_right = reverse_function(to_single_float(cotangent))
        return (total_grad + grad_right, (layer_output.astype(jnp.bfloat16), grad_in.astype(jnp.bfloat16)))
    total_grad, (layer_outputs, input_gradients) = lax.scan(group_step, jnp.zeros((2, ADAPTER_RANK, MODEL_WIDTH), jnp.float32), (inputs_all, grads_all, live_all))
    return (layer_outputs.reshape(ITEMS, L, MODEL_WIDTH), input_gradients.reshape(ITEMS, L, MODEL_WIDTH), total_grad / math.sqrt(TOKENS))
```

```python
import math

import jax
import jax.numpy as jnp
from jax import lax
from jax.experimental import pallas as pl
from jax.experimental.pallas import tpu as pltpu
from jax.sharding import Mesh, PartitionSpec as P

D = 768
HD = 64
RANK = 8
L = 512
FF = 3072
F32 = jnp.float32
BF = jnp.bfloat16

NF = 8
NR = 4
FB = D // NF
RB = D // NR
GH = RB // HD
VMEM = 60 << 20

DOWN0 = 64
ATTN0 = 80
GAIN0 = 83
SHIFT0 = 85
INB0 = 87
BACKB0 = 91


def mm(a, b):
    return jnp.dot(a, b, preferred_element_type=F32)


def mm_nt(a, b):
    return lax.dot_general(a, b, (((1,), (1,)), ((), ())), preferred_element_type=F32)


def lanes(rows):
    return lax.broadcasted_iota(jnp.int32, (rows, 128), 1)


def params(n):
    return pltpu.CompilerParams(dimension_semantics=("arbitrary",) * n, vmem_limit_bytes=VMEM)


def whole_spec(*shape):
    return pl.BlockSpec(shape, lambda *_: (0,) * len(shape), pipeline_mode=pl.Buffered(1))


def pack_first(w, attn, down, gain, shift, in_bias, back_bias):
    small = jnp.concatenate(
        [down[0], down[1], attn.T, gain.T, shift.T, in_bias.reshape(FF // D, FB).T, back_bias[:, None]], axis=1
    )
    small = jnp.pad(small, ((0, 0), (0, 64 - small.shape[1])))
    return jnp.stack(
        [
            w[0, :, :128],
            w[1, :, :128],
            w[2, :, :128],
            jnp.concatenate([w[0, :, 128:], w[1, :, 128:]], axis=1),
            jnp.concatenate([w[2, :, 128:], small], axis=1),
        ]
    )


def pack_rest(wo, wi, wb):
    b = wb.reshape(4, FB, RB)
    tiles = [wi[:, 128 * j : 128 * j + 128] for j in range(6)]
    tiles += [wo[:, :128]] + [b[j, :, :128] for j in range(4)]
    halves = [wo[:, 128:]] + [b[j, :, 128:] for j in range(4)]
    halves.append(halves[-1])
    tiles += [jnp.concatenate(halves[2 * j : 2 * j + 2], axis=1) for j in range(3)]
    return jnp.stack(tiles)


def small_body(meta, a_ref, b_ref, up_ref, upb_ref, sm_ref, vec_ref, inb_ref, scr):
    for j in range(4):
        scr[pl.ds(pl.multiple_of(meta[j], 32), FB), :] = a_ref[j, 0]
        scr[pl.ds(pl.multiple_of(meta[4 + j], 32), FB), :] = b_ref[j, 0]
    sm = scr[...]
    lane = lanes(D)
    sm_ref[...] = jnp.where(jnp.logical_and(lane >= DOWN0, lane < DOWN0 + 2 * RANK), sm, jnp.zeros((), BF))
    t = sm.astype(F32).T
    row = lambda i: t[i : i + 1]
    zero = jnp.zeros((1, D), F32)
    vec_ref[...] = jnp.concatenate(
        [row(ATTN0 + 2), row(GAIN0), row(SHIFT0), row(BACKB0), row(GAIN0 + 1), row(SHIFT0 + 1), zero, zero], axis=0
    )
    inb_ref[...] = t[INB0 : INB0 + 4]
    z = meta[8]
    zb = jnp.zeros((RANK, D), F32)
    for k in range(2):
        b = up_ref[k].astype(F32) * 2.0
        body = [jnp.zeros((DOWN0, D), F32)] + ([b, zb] if k == 0 else [zb, b])
        bias = jnp.broadcast_to(row(ATTN0 + k), (RANK, D))
        keep = lax.broadcasted_iota(jnp.int32, (RANK, D), 0) == 0
        body.append(jnp.where(keep, bias, 0.0))
        body.append(jnp.zeros((128 - DOWN0 - 3 * RANK, D), F32))
        full = jnp.concatenate(body, axis=0).astype(BF)
        for r in range(NR):
            part = full[:, RB * r : RB * r + RB]
            upb_ref[r ^ z, k] = jnp.concatenate([part, jnp.zeros((128, 256 - RB), BF)], axis=1)


def small_params(meta, a, b, up):
    tile = pl.BlockSpec((4, 1, FB, 128), lambda i, *_: (0, 4, 0, 0))
    return pl.pallas_call(
        small_body,
        grid_spec=pltpu.PrefetchScalarGridSpec(
            num_scalar_prefetch=1,
            grid=(1,),
            in_specs=[tile, tile, whole_spec(2, RANK, D)],
            out_specs=[whole_spec(NR, 2, 128, 256), whole_spec(D, 128), whole_spec(8, D), whole_spec(4, D)],
            scratch_shapes=[pltpu.VMEM((D, 128), BF)],
        ),
        out_shape=[
            jax.ShapeDtypeStruct((NR, 2, 128, 256), BF),
            jax.ShapeDtypeStruct((D, 128), BF),
            jax.ShapeDtypeStruct((8, D), F32),
            jax.ShapeDtypeStruct((4, D), F32),
        ],
        compiler_params=params(1),
        name="small_params",
    )(meta, a, b, up)


def attn_fwd_body(meta, x_ref, a_ref, b_ref, upb_ref, *refs):
    w_ref, q_ref, k_ref, v_ref, p_ref, o_ref, li_ref, u_ref = refs[-8:]
    i = pl.program_id(0)

    @pl.when(i == 0)
    def _():
        left = lanes(FB) < 64
        for src, base in ((a_ref, 0), (b_ref, 4)):
            for j in range(4):
                rows = pl.ds(pl.multiple_of(meta[base + j], 32), FB)
                for k in range(3):
                    w_ref[0, k, rows, :128] = src[j, k]
                t3 = src[j, 3]
                t4 = src[j, 4]
                w_ref[0, 0, rows, 128:] = jnp.where(left, t3, t4)
                w_ref[0, 1, rows, 128:] = jnp.concatenate([t3[:, 64:], t3[:, :64]], axis=1)
                w_ref[0, 2, rows, 128:] = t4

    x = x_ref[0]
    lane = lanes(L)
    raw = mm(x, w_ref[0, 0])
    u = raw[:, 128:].astype(BF)
    u = jnp.where(jnp.logical_and(lane >= DOWN0, lane < DOWN0 + 2 * RANK), u, jnp.zeros((), BF))
    u_ref[0] = u
    ua = jnp.where(lane == ATTN0, jnp.ones((), BF), u)
    q = (raw + mm(ua, upb_ref[0, 0])).astype(BF) * jnp.asarray(0.125, BF)
    k = mm(x, w_ref[0, 1]).astype(BF)
    v = (mm(x, w_ref[0, 2]) + mm(ua, upb_ref[0, 1])).astype(BF)
    live = meta[16 + 2 * i] + meta[17 + 2 * i]
    mask = jnp.where(lax.broadcasted_iota(jnp.int32, (1, L), 1) < live, 0.0, -1e30)
    left = lane < HD
    zero = jnp.zeros((), BF)
    one = jnp.ones((), BF)
    for t in range(2):
        c = slice(128 * t, 128 * t + 128)
        qp, kp, vp = q[:, c], k[:, c], v[:, c]
        q_ref[0, 0, t] = qp
        k_ref[0, 0, t] = kp
        v_ref[0, 0, t] = vp
        acc = None
        for h in range(2 * t, min(2 * t + 2, GH)):
            own = left if h % 2 == 0 else jnp.logical_not(left)
            s = mm_nt(qp, jnp.where(own, kp, zero)) + mask
            m = jnp.max(s, axis=1, keepdims=True)
            pb = jnp.exp(s - m).astype(BF)
            p_ref[0, 0, h] = pb
            rhs = jnp.concatenate([jnp.where(own, vp, zero), jnp.where(own, one, zero)], axis=1)
            part = mm(pb, rhs)
            acc = part if acc is None else acc + part
        total = acc[:, 128:]
        if 2 * t + 1 >= GH:
            total = jnp.where(left, total, 1.0)
        li = 1.0 / total
        li_ref[0, 0, t] = li
        o_ref[0, 0, t] = (acc[:, :128] * li).astype(BF)


def attn_fwd(group, meta, x, a, b, upb, kept):
    n = x.shape[0]
    shapes = [
        ((NR, 3, D, 256), BF),
        ((NR, n, 2, L, 128), BF),
        ((NR, n, 2, L, 128), BF),
        ((NR, n, 2, L, 128), BF),
        ((NR, n, GH, L, L), BF),
        ((NR, n, 2, L, 128), BF),
        ((NR, n, 2, L, 128), F32),
    ]
    specs = [pl.BlockSpec((1, 3, D, 256), lambda i, *_: (group, 0, 0, 0), pipeline_mode=pl.Buffered(1))]
    specs += [pl.BlockSpec((1, 1) + s[2:], lambda i, *_: (group, i, 0, 0, 0)) for s, _ in shapes[1:]]
    specs.append(pl.BlockSpec((1, L, 128), lambda i, *_: (i, 0, 0)))
    out_shape = [jax.ShapeDtypeStruct(s, d) for s, d in shapes] + [jax.ShapeDtypeStruct((n, L, 128), BF)]
    return pl.pallas_call(
        attn_fwd_body,
        grid_spec=pltpu.PrefetchScalarGridSpec(
            num_scalar_prefetch=1,
            grid=(n,),
            in_specs=[
                pl.BlockSpec((1, L, D), lambda i, *_: (i, 0, 0)),
                whole_spec(4, 5, FB, 128),
                whole_spec(4, 5, FB, 128),
                pl.BlockSpec((1, 2, 128, 256), lambda i, *_: (group, 0, 0, 0), pipeline_mode=pl.Buffered(1)),
            ]
            + [pl.BlockSpec(memory_space=pl.ANY)] * len(kept),
            out_specs=specs,
        ),
        out_shape=out_shape,
        input_output_aliases={5 + j: j for j in range(len(kept))},
        compiler_params=params(1),
        name="attn_fwd",
    )(meta, x, a, b, upb, *kept)


GP = 0.3275911 * math.sqrt(0.5)
GA = [0.5 * c for c in (0.254829592, -0.284496736, 1.421413741, -1.453152027, 1.061405429)]
GC = 1.0 / math.sqrt(2.0 * math.pi)


def gelu_pair(z):
    t = 1.0 / (1.0 + GP * jnp.abs(z))
    e = jnp.exp(-0.5 * z * z)
    tail = t * (GA[0] + t * (GA[1] + t * (GA[2] + t * (GA[3] + t * GA[4])))) * e
    cdf = jnp.where(z > 0, 1.0 - tail, tail)
    return z * cdf, cdf + z * (GC * e)


def ln_stats(v):
    c = v - jnp.mean(v, axis=-1, keepdims=True)
    r = lax.rsqrt(jnp.mean(c * c, axis=-1, keepdims=True) + 1e-5)
    return c * r, r


def ln_back(g, n, r, w):
    c = g * w
    return r * (c - jnp.mean(c, axis=-1, keepdims=True) - n * jnp.mean(c * n, axis=-1, keepdims=True))


TT = 256
FC = 512


def ffn_body(meta, x_ref, g_ref, o_ref, li_ref, r_ref, vec_ref, bi_ref, ho_ref, gf_ref, dm_ref,
             wo_scr, wi_scr, wb_scr, act_scr, dact_scr, gi_scr):
    @pl.when(jnp.logical_and(pl.program_id(0) == 0, pl.program_id(1) == 0))
    def _():
        z = meta[8]

        def block(f, carry):
            rows = pl.ds(pl.multiple_of(f * FB, 32), FB)
            tile = lambda r, j: r_ref[NR * f + r, j]
            left = lambda r, j: r_ref[NR * f + r, j, :, :64]
            right = lambda r, j: r_ref[NR * f + r, j, :, 64:]
            for r in range(NR):
                for j in range(6):
                    wi_scr[rows, pl.ds(D * r + 128 * j, 128)] = tile(r, j)
            slot = ((f // 2) ^ z) * 2 + f % 2
            wo_scr[pl.ds(pl.multiple_of(slot * FB, 32), FB), :] = jnp.concatenate(
                sum([[tile(r, 6), left(r, 11)] for r in range(NR)], []), axis=1
            )
            for j in range(4):
                half = (right if j % 2 == 0 else left)
                wb_scr[pl.ds(pl.multiple_of(f * 4 * FB + j * FB, 32), FB), :] = jnp.concatenate(
                    sum([[tile(r, 7 + j), half(r, 11 + (j + 1) // 2)] for r in range(NR)], []), axis=1
                )
            return carry

        lax.fori_loop(0, NF, block, 0)

    x = x_ref[0].astype(F32)
    mixed = jnp.concatenate(sum([[o_ref[g, 0, 0], o_ref[g, 0, 1][:, :64]] for g in range(NR)], []), axis=1)
    n1, r1 = ln_stats(x + mm(mixed, wo_scr[...]) + vec_ref[0:1])
    h1 = n1 * vec_ref[1:2] + vec_ref[2:3]
    h1b = h1.astype(BF)
    for c in range(FF // FC):
        s = pl.ds(c * FC, FC)
        a, d = gelu_pair(mm(h1b, wi_scr[:, s]) + bi_ref[0:1, s])
        act_scr[:, s] = a.astype(BF)
        dact_scr[:, s] = d.astype(BF)
    n2, r2 = ln_stats(h1 + mm(act_scr[...], wb_scr[...]) + vec_ref[3:4])
    ho_ref[0] = (n2 * vec_ref[4:5] + vec_ref[5:6]).astype(BF)
    gs = ln_back(g_ref[0].astype(F32), n2, r2, vec_ref[4:5])
    gsb = gs.astype(BF)
    for c in range(FF // FC):
        s = pl.ds(c * FC, FC)
        ga = mm_nt(gsb, wb_scr[s, :])
        gi_scr[:, s] = (ga * dact_scr[:, s].astype(F32)).astype(BF)
    gh = gs + mm_nt(gi_scr[...], wi_scr[...])
    gf = ln_back(gh, n1, r1, vec_ref[1:2])
    gf_ref[0] = gf
    gm = mm_nt(gf.astype(BF), wo_scr[...])
    for g in range(NR):
        part = gm[:, RB * g : RB * g + RB]
        dm_ref[g, 0, 0] = (part[:, :128] * li_ref[g, 0, 0]).astype(BF)
        tail = part[:, 128:] * li_ref[g, 0, 1][:, :64]
        dm_ref[g, 0, 1] = jnp.concatenate([tail, jnp.zeros((TT, 64), F32)], axis=1).astype(BF)


def ffn(meta, x, g, o, li, rest, vec, bi):
    n = x.shape[0]
    row = pl.BlockSpec((1, TT, D), lambda i, t, *_: (i, t, 0))
    prow = pl.BlockSpec((NR, 1, 2, TT, 128), lambda i, t, *_: (0, i, 0, t, 0))
    return pl.pallas_call(
        ffn_body,
        grid_spec=pltpu.PrefetchScalarGridSpec(
            num_scalar_prefetch=1,
            grid=(n, L // TT),
            in_specs=[row, row, prow, prow, whole_spec(NF * NR, 14, FB, 128), whole_spec(8, D), whole_spec(1, FF)],
            out_specs=[row, row, prow],
            scratch_shapes=[pltpu.VMEM((D, D), BF), pltpu.VMEM((D, FF), BF), pltpu.VMEM((FF, D), BF)]
            + [pltpu.VMEM((TT, FF), BF)] * 3,
        ),
        out_shape=[
            jax.ShapeDtypeStruct((n, L, D), BF),
            jax.ShapeDtypeStruct((n, L, D), F32),
            jax.ShapeDtypeStruct((NR, n, 2, L, 128), BF),
        ],
        compiler_params=params(2),
        name="ffn",
    )(meta, x, g, o, li, rest, vec, bi)


def attn_bwd_body(meta, q_ref, k_ref, v_ref, p_ref, o_ref, dm_ref, gf_ref, u_ref, w_ref, sm_ref, upb_ref,
                  hg_ref, ag_ref, w_scr, up_scr, acc_scr, dq_scr, dkt_scr, dvt_scr):
    i = pl.program_id(0)
    cat = lambda parts: jnp.concatenate(parts, axis=1)

    @pl.when(i == 0)
    def _():
        for k in range(3):
            w_scr[k] = cat([w_ref[g, k][:, :RB] for g in range(NR)])
        for k in range(2):
            up_scr[k] = cat([upb_ref[g, k][:, :RB] for g in range(NR)])
        acc_scr[...] = jnp.zeros_like(acc_scr)

    def group(g, carry):
        left = lanes(L) < HD
        zero = jnp.zeros((), BF)
        neg = jnp.asarray(-1.0, BF)
        for t in range(2):
            qp, kp, vp = q_ref[g, 0, t], k_ref[g, 0, t], v_ref[g, 0, t]
            dm = dm_ref[g, 0, t]
            lhs = jnp.concatenate([dm, dm * o_ref[g, 0, t]], axis=1)
            qt = qp.T
            dmt = dm.T
            dq = None
            for h in range(2 * t, min(2 * t + 2, GH)):
                own = left if h % 2 == 0 else jnp.logical_not(left)
                rhs = jnp.concatenate([jnp.where(own, vp, zero), jnp.where(own, neg, zero)], axis=1)
                p = p_ref[g, 0, h]
                ds = (p.astype(F32) * mm_nt(lhs, rhs)).astype(BF)
                part = mm(ds, jnp.where(own, kp, zero))
                dq = part if dq is None else dq + part
                src = slice(HD * (h % 2), HD * (h % 2) + HD)
                dst = slice(HD * h, HD * h + HD)
                dkt_scr[g, dst, :] = mm(qt[src, :], ds).astype(BF)
                dvt_scr[g, dst, :] = mm(dmt[src, :], p).astype(BF)
            dq_scr[g, t] = (dq * 0.125).astype(BF)
        return carry

    lax.fori_loop(0, NR, group, 0)
    dq = cat(sum([[dq_scr[g, 0], dq_scr[g, 1][:, :64]] for g in range(NR)], []))
    dk = cat([dkt_scr[g].T for g in range(NR)])
    dv = cat([dvt_scr[g].T for g in range(NR)])
    gu = (mm_nt(dq, up_scr[0]) + mm_nt(dv, up_scr[1])).astype(BF)
    hg = gf_ref[0] + mm_nt(dq, w_scr[0]) + mm_nt(dk, w_scr[1]) + mm_nt(dv, w_scr[2]) + mm_nt(gu, sm_ref[...])
    hg_ref[0] = hg.astype(BF)
    ut = u_ref[0].T
    acc_scr[0] += mm(ut[DOWN0 : DOWN0 + RANK], dq)
    acc_scr[1] += mm(ut[DOWN0 + RANK : DOWN0 + 2 * RANK], dv)

    @pl.when(i == pl.num_programs(0) - 1)
    def _():
        for g in range(NR):
            ag_ref[g ^ meta[8]] = acc_scr[:, :, RB * g : RB * g + RB]


def attn_bwd(meta, q, k, v, p, o, dm, gf, u, w, sm, upb):
    n = gf.shape[0]
    tile = pl.BlockSpec((NR, 1, 2, L, 128), lambda i, *_: (0, i, 0, 0, 0))
    return pl.pallas_call(
        attn_bwd_body,
        grid_spec=pltpu.PrefetchScalarGridSpec(
            num_scalar_prefetch=1,
            grid=(n,),
            in_specs=[tile] * 3
            + [pl.BlockSpec((NR, 1, GH, L, L), lambda i, *_: (0, i, 0, 0, 0))]
            + [tile] * 2
            + [
                pl.BlockSpec((1, L, D), lambda i, *_: (i, 0, 0)),
                pl.BlockSpec((1, L, 128), lambda i, *_: (i, 0, 0)),
                whole_spec(NR, 3, D, 256),
                whole_spec(D, 128),
                whole_spec(NR, 2, 128, 256),
            ],
            out_specs=[pl.BlockSpec((1, L, D), lambda i, *_: (i, 0, 0)), whole_spec(NR, 2, RANK, RB)],
            scratch_shapes=[
                pltpu.VMEM((3, D, D), BF),
                pltpu.VMEM((2, 128, D), BF),
                pltpu.VMEM((2, RANK, D), F32),
                pltpu.VMEM((NR, 2, L, 128), BF),
                pltpu.VMEM((NR, RB, L), BF),
                pltpu.VMEM((NR, RB, L), BF),
            ],
        ),
        out_shape=[jax.ShapeDtypeStruct((n, L, D), BF), jax.ShapeDtypeStruct((NR, 2, RANK, RB), F32)],
        compiler_params=params(1),
        name="attn_bwd",
    )(meta, q, k, v, p, o, dm, gf, u, w, sm, upb)


def layer(meta, x, g, up, firsts, rest):
    upb, sm, vec, inb = small_params(meta, firsts[0][0], firsts[0][1], up)
    kept = ()
    for group in range(NR):
        a, b = firsts[group]
        out = attn_fwd(group, meta, x, a, b, upb, kept)
        kept, u = out[:-1], out[-1]
    w, q, k, v, p, o, li = kept
    bi = inb.reshape(4, NF, FB).transpose(1, 0, 2).reshape(1, FF)
    ho, gf, dm = ffn(meta, x, g, o, li, rest, vec, bi)
    hg, ag = attn_bwd(meta, q, k, v, p, o, dm, gf, u, w, sm, upb)
    return ho, hg, ag


def finish(ag, tokens):
    return ag.transpose(1, 2, 0, 3).reshape(2, RANK, D) * (2.0 / math.sqrt(tokens))


def meta_of(y, x, c, z, lens):
    rows = []
    for core in (c, 1 - c):
        for dy in range(2):
            for dx in range(2):
                rows.append((((y ^ dy) * 2 + (x ^ dx)) * 2 + core) * FB)
    head = jnp.stack([jnp.asarray(v, jnp.int32) for v in rows + [z] + [0] * 7])
    return jnp.concatenate([head, lens.reshape(-1)])


def block_blocks(qkv, wo, wi, wb, attn, down, gain, shift, inb, backb):
    def first(f, r):
        rows, cols = slice(FB * f, FB * f + FB), slice(RB * r, RB * r + RB)
        wide = slice(4 * FB * f, 4 * FB * f + 4 * FB)
        return pack_first(
            qkv[:, rows, cols], attn[:, rows], down[:, rows], gain[:, rows], shift[:, rows], inb[wide], backb[rows]
        )

    def other(f, r):
        rows, cols = slice(FB * f, FB * f + FB), slice(RB * r, RB * r + RB)
        return pack_rest(
            wo[rows, cols], wi[rows, D * r : D * r + D], wb[4 * FB * f : 4 * FB * f + 4 * FB, cols]
        )

    firsts = [
        tuple(jnp.stack([first(2 * j + core, r) for j in range(4)]) for core in range(2)) for r in range(NR)
    ]
    return firsts, jnp.stack([other(f, r) for f in range(NF) for r in range(NR)])


def device_plain(x, lens, qkv, wo, attn, down, up, gain, shift, wi, inb, wb, backb, g):
    tokens = x.shape[0] * L * lax.axis_size("fsdp") * lax.axis_size("rep")
    gather = lambda a, axis, dim: lax.all_gather(a, axis, axis=dim, tiled=True)
    both = lambda a, row, col: gather(gather(a, "rep", col), "fsdp", row)
    firsts, rest = block_blocks(
        both(qkv, 1, 2), both(wo, 0, 1), both(wi, 0, 1), both(wb, 0, 1),
        gather(attn, "fsdp", 1), gather(down, "fsdp", 1), gather(gain, "fsdp", 1), gather(shift, "fsdp", 1),
        gather(inb, "fsdp", 0), gather(backb, "fsdp", 0),
    )
    ho, hg, ag = layer(meta_of(0, 0, 0, 0, lens), x, g, up, firsts, rest)
    return ho, hg, finish(lax.psum(ag, ("fsdp", "rep")), tokens)


AXES = ("y", "x", "c", "z")


def flip(value, dy=0, dx=0, dc=0, dz=0):
    pairs = []
    for i in range(32):
        y, x, c, z = i >> 4, (i >> 3) & 1, (i >> 2) & 1, i & 3
        pairs.append((i, ((y ^ dy) << 4) | ((x ^ dx) << 3) | ((c ^ dc) << 2) | (z ^ dz)))
    return lax.ppermute(value, AXES, pairs)


def device_block(x, lens, qkv, wo, attn, down, up, gain, shift, wi, inb, wb, backb, g):
    tokens = x.shape[0] * L * 32
    own = pack_first(qkv, attn, down, gain, shift, inb, backb)
    near = jnp.stack([own, flip(own, dx=1), flip(own, dy=1), flip(own, dy=1, dx=1)])
    firsts = [(near, flip(near, dc=1))]
    for k in range(1, NR):
        far = flip(near, dz=k)
        firsts.append((far, flip(far, dc=1)))
    rest = lax.all_gather(pack_rest(wo, wi, wb), AXES, axis=0)
    meta = meta_of(lax.axis_index("y"), lax.axis_index("x"), lax.axis_index("c"), lax.axis_index("z"), lens)
    ho, hg, ag = layer(meta, x, g, up, firsts, rest)
    for step in (dict(dc=1), dict(dx=1), dict(dy=1), dict(dz=1), dict(dz=2)):
        ag = ag + flip(ag, **step)
    return ho, hg, finish(ag, tokens)


def solution(mesh):
    if mesh.shape["fsdp"] == NF and mesh.shape["rep"] == NR:
        mesh = Mesh(mesh.devices.reshape(2, 2, 2, 4), AXES)
        body, f, r = device_block, ("y", "x", "c"), ("z",)
    else:
        body, f, r = device_plain, ("fsdp",), ("rep",)
    items = P(f + r, None, None)
    in_specs = (
        items,
        P(f + r, None),
        P(None, f, r),
        P(f, r),
        P(None, f),
        P(None, f, None),
        P(),
        P(None, f),
        P(None, f),
        P(f, r),
        P(f),
        P(f, r),
        P(f),
        items,
    )

    def call(layer_input, lens, qkv, wo, attn, down, up, gain, shift, wi, inb, wb, backb, g):
        return jax.shard_map(
            body, mesh=mesh, in_specs=in_specs, out_specs=(items, items, P()), check_vma=False
        )(layer_input, lens, qkv, wo, attn, down, up, gain, shift, wi, inb, wb, backb, g)

    return call
```

```python
import math

import jax
import jax.numpy as jnp
from jax import lax
from jax.experimental import pallas as pl
from jax.experimental.pallas import tpu as pltpu
from jax.sharding import Mesh, PartitionSpec as P

D = 768
HD = 64
RANK = 8
L = 512
FF = 3072
F32 = jnp.float32
BF = jnp.bfloat16

NF = 8
NR = 4
FB = D // NF
RB = D // NR
GH = RB // HD
VMEM = 60 << 20

DOWN0 = 64
ATTN0 = 80
GAIN0 = 83
SHIFT0 = 85
INB0 = 87
BACKB0 = 91


def mm(a, b):
    return jnp.dot(a, b, preferred_element_type=F32)


def mm_nt(a, b):
    return lax.dot_general(a, b, (((1,), (1,)), ((), ())), preferred_element_type=F32)


def lanes(rows):
    return lax.broadcasted_iota(jnp.int32, (rows, 128), 1)


def params(n):
    return pltpu.CompilerParams(dimension_semantics=("arbitrary",) * n, vmem_limit_bytes=VMEM)


def whole_spec(*shape):
    return pl.BlockSpec(shape, lambda *_: (0,) * len(shape), pipeline_mode=pl.Buffered(1))


def pack_body(qkv_ref, attn_ref, down_ref, gain_ref, shift_ref, inb_ref, backb_ref, wo_ref, wi_ref, wb_ref,
              first_ref, rest_ref, scr):
    scr[...] = jnp.zeros_like(scr)
    up = lambda v: v.astype(F32)
    for k in range(2):
        scr[pl.ds(DOWN0 + RANK * k, RANK), :FB] = up(down_ref[k])
    inb = up(inb_ref[...])
    rows = [up(attn_ref[...]), up(gain_ref[...]), up(shift_ref[...])]
    rows += [inb[:, FB * j : FB * j + FB] for j in range(FF // D)] + [up(backb_ref[...])]
    at = ATTN0
    for v in rows:
        scr[pl.ds(at, v.shape[0]), :FB] = v
        at += v.shape[0]
    small = scr[...].T[:FB, 64:].astype(BF)
    for k in range(3):
        first_ref[k] = qkv_ref[k, :, :128]
    first_ref[3] = jnp.concatenate([qkv_ref[0, :, 128:], qkv_ref[1, :, 128:]], axis=1)
    first_ref[4] = jnp.concatenate([qkv_ref[2, :, 128:], small], axis=1)
    for j in range(6):
        rest_ref[j] = wi_ref[:, 128 * j : 128 * j + 128]
    rest_ref[6] = wo_ref[:, :128]
    rest_ref[7] = jnp.concatenate([wo_ref[:, 128:], wo_ref[:, 128:]], axis=1)
    for h in range(2):
        for j in range(3):
            rest_ref[8 + 3 * h + j] = wb_ref[FB * h : FB * h + FB, 128 * j : 128 * j + 128]


def pack(qkv, attn, down, gain, shift, inb, backb, wo, wi, wb):
    return pl.pallas_call(
        pack_body,
        out_shape=[jax.ShapeDtypeStruct((5, FB, 128), BF), jax.ShapeDtypeStruct((14, FB, 128), BF)],
        scratch_shapes=[pltpu.VMEM((128, 128), F32)],
        compiler_params=pltpu.CompilerParams(vmem_limit_bytes=VMEM),
        name="pack",
    )(qkv, attn, down.transpose(0, 2, 1), gain, shift, inb[None], backb[None], wo, wi, wb.T)


def small_body(meta, a_ref, b_ref, up_ref, upb_ref, sm_ref, vec_ref, inb_ref, scr):
    for j in range(4):
        scr[pl.ds(pl.multiple_of(meta[j], 32), FB), :] = a_ref[j, 0]
        scr[pl.ds(pl.multiple_of(meta[4 + j], 32), FB), :] = b_ref[j, 0]
    sm = scr[...]
    lane = lanes(D)
    sm_ref[...] = jnp.where(jnp.logical_and(lane >= DOWN0, lane < DOWN0 + 2 * RANK), sm, jnp.zeros((), BF))
    t = sm.astype(F32).T
    row = lambda i: t[i : i + 1]
    zero = jnp.zeros((1, D), F32)
    vec_ref[...] = jnp.concatenate(
        [row(ATTN0 + 2), row(GAIN0), row(SHIFT0), row(BACKB0), row(GAIN0 + 1), row(SHIFT0 + 1), zero, zero], axis=0
    )
    inb_ref[...] = jnp.concatenate(
        [t[INB0 + j : INB0 + j + 1, FB * f : FB * f + FB] for f in range(NF) for j in range(4)], axis=1
    )
    z = meta[8]
    zb = jnp.zeros((RANK, D), F32)
    for k in range(2):
        b = up_ref[k].astype(F32) * 2.0
        body = [jnp.zeros((DOWN0, D), F32)] + ([b, zb] if k == 0 else [zb, b])
        bias = jnp.broadcast_to(row(ATTN0 + k), (RANK, D))
        keep = lax.broadcasted_iota(jnp.int32, (RANK, D), 0) == 0
        body.append(jnp.where(keep, bias, 0.0))
        body.append(jnp.zeros((128 - DOWN0 - 3 * RANK, D), F32))
        full = jnp.concatenate(body, axis=0).astype(BF)
        for r in range(NR):
            part = full[:, RB * r : RB * r + RB]
            upb_ref[(z + NR - r) % NR, k] = jnp.concatenate([part, jnp.zeros((128, 256 - RB), BF)], axis=1)


def small_params(meta, a, b, up):
    tile = pl.BlockSpec((4, 1, FB, 128), lambda i, *_: (0, 4, 0, 0))
    return pl.pallas_call(
        small_body,
        grid_spec=pltpu.PrefetchScalarGridSpec(
            num_scalar_prefetch=1,
            grid=(1,),
            in_specs=[tile, tile, whole_spec(2, RANK, D)],
            out_specs=[whole_spec(NR, 2, 128, 256), whole_spec(D, 128), whole_spec(8, D), whole_spec(1, FF)],
            scratch_shapes=[pltpu.VMEM((D, 128), BF)],
        ),
        out_shape=[
            jax.ShapeDtypeStruct((NR, 2, 128, 256), BF),
            jax.ShapeDtypeStruct((D, 128), BF),
            jax.ShapeDtypeStruct((8, D), F32),
            jax.ShapeDtypeStruct((1, FF), F32),
        ],
        compiler_params=params(1),
        name="small_params",
    )(meta, a, b, up)


def attn_fwd_body(meta, x_ref, a_ref, b_ref, upb_ref, *refs):
    w_ref, q_ref, k_ref, v_ref, p_ref, o_ref, li_ref, u_ref = refs[-8:]
    i = pl.program_id(0)

    @pl.when(i == 0)
    def _():
        left = lanes(FB) < 64
        for src, base in ((a_ref, 0), (b_ref, 4)):
            for j in range(4):
                rows = pl.ds(pl.multiple_of(meta[base + j], 32), FB)
                for k in range(3):
                    w_ref[0, k, rows, :128] = src[j, k]
                t3 = src[j, 3]
                t4 = src[j, 4]
                w_ref[0, 0, rows, 128:] = jnp.where(left, t3, t4)
                w_ref[0, 1, rows, 128:] = jnp.concatenate([t3[:, 64:], t3[:, :64]], axis=1)
                w_ref[0, 2, rows, 128:] = t4

    x = x_ref[0]
    lane = lanes(L)
    raw = mm(x, w_ref[0, 0])
    u = raw[:, 128:].astype(BF)
    u = jnp.where(jnp.logical_and(lane >= DOWN0, lane < DOWN0 + 2 * RANK), u, jnp.zeros((), BF))
    u_ref[0] = u
    ua = jnp.where(lane == ATTN0, jnp.ones((), BF), u)
    q = (raw + mm(ua, upb_ref[0, 0])).astype(BF) * jnp.asarray(0.125, BF)
    k = mm(x, w_ref[0, 1]).astype(BF)
    v = (mm(x, w_ref[0, 2]) + mm(ua, upb_ref[0, 1])).astype(BF)
    live = meta[16 + 2 * i] + meta[17 + 2 * i]
    mask = jnp.where(lax.broadcasted_iota(jnp.int32, (1, L), 1) < live, 0.0, -1e30)
    left = lane < HD
    zero = jnp.zeros((), BF)
    one = jnp.ones((), BF)
    for t in range(2):
        c = slice(128 * t, 128 * t + 128)
        qp, kp, vp = q[:, c], k[:, c], v[:, c]
        q_ref[0, 0, t] = qp
        k_ref[0, 0, t] = kp
        v_ref[0, 0, t] = vp
        acc = None
        for h in range(2 * t, min(2 * t + 2, GH)):
            own = left if h % 2 == 0 else jnp.logical_not(left)
            s = mm_nt(qp, jnp.where(own, kp, zero)) + mask
            m = jnp.max(s, axis=1, keepdims=True)
            pb = jnp.exp(s - m).astype(BF)
            p_ref[0, 0, h] = pb
            rhs = jnp.concatenate([jnp.where(own, vp, zero), jnp.where(own, one, zero)], axis=1)
            part = mm(pb, rhs)
            acc = part if acc is None else acc + part
        total = acc[:, 128:]
        if 2 * t + 1 >= GH:
            total = jnp.where(left, total, 1.0)
        li = 1.0 / total
        li_ref[0, 0, t] = li
        o_ref[0, 0, t] = (acc[:, :128] * li).astype(BF)


def attn_fwd(group, meta, x, a, b, upb, kept):
    n = x.shape[0]
    shapes = [
        ((NR, 3, D, 256), BF),
        ((NR, n, 2, L, 128), BF),
        ((NR, n, 2, L, 128), BF),
        ((NR, n, 2, L, 128), BF),
        ((NR, n, GH, L, L), BF),
        ((NR, n, 2, L, 128), BF),
        ((NR, n, 2, L, 128), F32),
    ]
    specs = [pl.BlockSpec((1, 3, D, 256), lambda i, *_: (group, 0, 0, 0), pipeline_mode=pl.Buffered(1))]
    specs += [pl.BlockSpec((1, 1) + s[2:], lambda i, *_: (group, i, 0, 0, 0)) for s, _ in shapes[1:]]
    specs.append(pl.BlockSpec((1, L, 128), lambda i, *_: (i, 0, 0)))
    out_shape = [jax.ShapeDtypeStruct(s, d) for s, d in shapes] + [jax.ShapeDtypeStruct((n, L, 128), BF)]
    return pl.pallas_call(
        attn_fwd_body,
        grid_spec=pltpu.PrefetchScalarGridSpec(
            num_scalar_prefetch=1,
            grid=(n,),
            in_specs=[
                pl.BlockSpec((1, L, D), lambda i, *_: (i, 0, 0)),
                whole_spec(4, 5, FB, 128),
                whole_spec(4, 5, FB, 128),
                pl.BlockSpec((1, 2, 128, 256), lambda i, *_: (group, 0, 0, 0), pipeline_mode=pl.Buffered(1)),
            ]
            + [pl.BlockSpec(memory_space=pl.ANY)] * len(kept),
            out_specs=specs,
        ),
        out_shape=out_shape,
        input_output_aliases={5 + j: j for j in range(len(kept))},
        compiler_params=params(1),
        name="attn_fwd",
    )(meta, x, a, b, upb, *kept)


GP = 0.3275911 * math.sqrt(0.5)
GA = [0.5 * c for c in (0.254829592, -0.284496736, 1.421413741, -1.453152027, 1.061405429)]
GC = 1.0 / math.sqrt(2.0 * math.pi)


def gelu_pair(z):
    t = 1.0 / (1.0 + GP * jnp.abs(z))
    e = jnp.exp(-0.5 * z * z)
    tail = t * (GA[0] + t * (GA[1] + t * (GA[2] + t * (GA[3] + t * GA[4])))) * e
    cdf = jnp.where(z > 0, 1.0 - tail, tail)
    return z * cdf, cdf + z * (GC * e)


def ln_stats(v):
    c = v - jnp.mean(v, axis=-1, keepdims=True)
    r = lax.rsqrt(jnp.mean(c * c, axis=-1, keepdims=True) + 1e-5)
    return c * r, r


def ln_back(g, n, r, w):
    c = g * w
    return r * (c - jnp.mean(c, axis=-1, keepdims=True) - n * jnp.mean(c * n, axis=-1, keepdims=True))


TT = 256
FC = 512


def ffn_body(meta, x_ref, g_ref, o_ref, li_ref, r_ref, vec_ref, bi_ref, ho_ref, gf_ref, dm_ref,
             wo_scr, wi_scr, wb_scr, act_scr, dact_scr, gi_scr):
    @pl.when(jnp.logical_and(pl.program_id(0) == 0, pl.program_id(1) == 0))
    def _():
        z = meta[8]

        def block(f, carry):
            rows = pl.ds(pl.multiple_of(f * FB, 32), FB)
            tile = lambda r, j: r_ref[NR * f + r, j]
            left = lambda r, j: r_ref[NR * f + r, j, :, :64]
            for r in range(NR):
                for j in range(6):
                    wi_scr[rows, pl.ds(D * r + 128 * j, 128)] = tile(r, j)
            slot = ((z + NR - f // 2) % NR) * 2 + f % 2
            wo_scr[pl.ds(pl.multiple_of(slot * FB, 32), FB), :] = jnp.concatenate(
                sum([[tile(r, 6), left(r, 7)] for r in range(NR)], []), axis=1
            )
            for r in range(NR):
                for h in range(2):
                    for j in range(3):
                        cols = pl.ds(pl.multiple_of(f * 4 * FB + 128 * j, 128), 128)
                        wb_scr[RB * r + FB * h : RB * r + FB * h + FB, cols] = tile(r, 8 + 3 * h + j)
            return carry

        lax.fori_loop(0, NF, block, 0)

    x = x_ref[0].astype(F32)
    mixed = jnp.concatenate(sum([[o_ref[g, 0, 0], o_ref[g, 0, 1][:, :64]] for g in range(NR)], []), axis=1)
    n1, r1 = ln_stats(x + mm(mixed, wo_scr[...]) + vec_ref[0:1])
    h1 = n1 * vec_ref[1:2] + vec_ref[2:3]
    h1b = h1.astype(BF)
    for c in range(FF // FC):
        s = pl.ds(c * FC, FC)
        a, d = gelu_pair(mm(h1b, wi_scr[:, s]) + bi_ref[0:1, s])
        act_scr[:, s] = a.astype(BF)
        dact_scr[:, s] = d.astype(BF)
    n2, r2 = ln_stats(h1 + mm_nt(act_scr[...], wb_scr[...]) + vec_ref[3:4])
    ho_ref[0] = (n2 * vec_ref[4:5] + vec_ref[5:6]).astype(BF)
    gs = ln_back(g_ref[0].astype(F32), n2, r2, vec_ref[4:5])
    gsb = gs.astype(BF)
    for c in range(FF // FC):
        s = pl.ds(c * FC, FC)
        ga = mm(gsb, wb_scr[:, s])
        gi_scr[:, s] = (ga * dact_scr[:, s].astype(F32)).astype(BF)
    gh = gs + mm_nt(gi_scr[...], wi_scr[...])
    gf = ln_back(gh, n1, r1, vec_ref[1:2])
    gf_ref[0] = gf
    gm = mm_nt(gf.astype(BF), wo_scr[...])
    for g in range(NR):
        part = gm[:, RB * g : RB * g + RB]
        dm_ref[g, 0, 0] = (part[:, :128] * li_ref[g, 0, 0]).astype(BF)
        tail = part[:, 128:] * li_ref[g, 0, 1][:, :64]
        dm_ref[g, 0, 1] = jnp.concatenate([tail, jnp.zeros((TT, 64), F32)], axis=1).astype(BF)


def ffn(meta, x, g, o, li, rest, vec, bi):
    n = x.shape[0]
    row = pl.BlockSpec((1, TT, D), lambda i, t, *_: (i, t, 0))
    prow = pl.BlockSpec((NR, 1, 2, TT, 128), lambda i, t, *_: (0, i, 0, t, 0))
    return pl.pallas_call(
        ffn_body,
        grid_spec=pltpu.PrefetchScalarGridSpec(
            num_scalar_prefetch=1,
            grid=(n, L // TT),
            in_specs=[row, row, prow, prow, whole_spec(NF * NR, 14, FB, 128), whole_spec(8, D), whole_spec(1, FF)],
            out_specs=[row, row, prow],
            scratch_shapes=[pltpu.VMEM((D, D), BF), pltpu.VMEM((D, FF), BF), pltpu.VMEM((D, FF), BF)]
            + [pltpu.VMEM((TT, FF), BF)] * 3,
        ),
        out_shape=[
            jax.ShapeDtypeStruct((n, L, D), BF),
            jax.ShapeDtypeStruct((n, L, D), F32),
            jax.ShapeDtypeStruct((NR, n, 2, L, 128), BF),
        ],
        compiler_params=params(2),
        name="ffn",
    )(meta, x, g, o, li, rest, vec, bi)


def attn_bwd_body(meta, q_ref, k_ref, v_ref, p_ref, o_ref, dm_ref, gf_ref, u_ref, w_ref, sm_ref, upb_ref,
                  hg_ref, ag_ref, w_scr, up_scr, acc_scr, dq_scr, dkt_scr, dvt_scr):
    i = pl.program_id(0)
    cat = lambda parts: jnp.concatenate(parts, axis=1)

    @pl.when(i == 0)
    def _():
        for k in range(3):
            w_scr[k] = cat([w_ref[g, k][:, :RB] for g in range(NR)])
        for k in range(2):
            up_scr[k] = cat([upb_ref[g, k][:, :RB] for g in range(NR)])
        acc_scr[...] = jnp.zeros_like(acc_scr)

    def group(g, carry):
        left = lanes(L) < HD
        zero = jnp.zeros((), BF)
        neg = jnp.asarray(-1.0, BF)
        for t in range(2):
            qp, kp, vp = q_ref[g, 0, t], k_ref[g, 0, t], v_ref[g, 0, t]
            dm = dm_ref[g, 0, t]
            lhs = jnp.concatenate([dm, dm * o_ref[g, 0, t]], axis=1)
            qt = qp.T
            dmt = dm.T
            dq = None
            for h in range(2 * t, min(2 * t + 2, GH)):
                own = left if h % 2 == 0 else jnp.logical_not(left)
                rhs = jnp.concatenate([jnp.where(own, vp, zero), jnp.where(own, neg, zero)], axis=1)
                p = p_ref[g, 0, h]
                ds = (p.astype(F32) * mm_nt(lhs, rhs)).astype(BF)
                part = mm(ds, jnp.where(own, kp, zero))
                dq = part if dq is None else dq + part
                src = slice(HD * (h % 2), HD * (h % 2) + HD)
                dst = slice(HD * h, HD * h + HD)
                dkt_scr[g, dst, :] = mm(qt[src, :], ds).astype(BF)
                dvt_scr[g, dst, :] = mm(dmt[src, :], p).astype(BF)
            dq_scr[g, t] = (dq * 0.125).astype(BF)
        return carry

    lax.fori_loop(0, NR, group, 0)
    dq = cat(sum([[dq_scr[g, 0], dq_scr[g, 1][:, :64]] for g in range(NR)], []))
    dk = cat([dkt_scr[g].T for g in range(NR)])
    dv = cat([dvt_scr[g].T for g in range(NR)])
    gu = (mm_nt(dq, up_scr[0]) + mm_nt(dv, up_scr[1])).astype(BF)
    hg = gf_ref[0] + mm_nt(dq, w_scr[0]) + mm_nt(dk, w_scr[1]) + mm_nt(dv, w_scr[2]) + mm_nt(gu, sm_ref[...])
    hg_ref[0] = hg.astype(BF)
    ut = u_ref[0].T
    acc_scr[0] += mm(ut[DOWN0 : DOWN0 + RANK], dq)
    acc_scr[1] += mm(ut[DOWN0 + RANK : DOWN0 + 2 * RANK], dv)

    @pl.when(i == pl.num_programs(0) - 1)
    def _():
        for g in range(NR):
            ag_ref[(meta[8] + NR - g) % NR] = acc_scr[:, :, RB * g : RB * g + RB]


def attn_bwd(meta, q, k, v, p, o, dm, gf, u, w, sm, upb):
    n = gf.shape[0]
    tile = pl.BlockSpec((NR, 1, 2, L, 128), lambda i, *_: (0, i, 0, 0, 0))
    return pl.pallas_call(
        attn_bwd_body,
        grid_spec=pltpu.PrefetchScalarGridSpec(
            num_scalar_prefetch=1,
            grid=(n,),
            in_specs=[tile] * 3
            + [pl.BlockSpec((NR, 1, GH, L, L), lambda i, *_: (0, i, 0, 0, 0))]
            + [tile] * 2
            + [
                pl.BlockSpec((1, L, D), lambda i, *_: (i, 0, 0)),
                pl.BlockSpec((1, L, 128), lambda i, *_: (i, 0, 0)),
                whole_spec(NR, 3, D, 256),
                whole_spec(D, 128),
                whole_spec(NR, 2, 128, 256),
            ],
            out_specs=[pl.BlockSpec((1, L, D), lambda i, *_: (i, 0, 0)), whole_spec(NR, 2, RANK, RB)],
            scratch_shapes=[
                pltpu.VMEM((3, D, D), BF),
                pltpu.VMEM((2, 128, D), BF),
                pltpu.VMEM((2, RANK, D), F32),
                pltpu.VMEM((NR, 2, L, 128), BF),
                pltpu.VMEM((NR, RB, L), BF),
                pltpu.VMEM((NR, RB, L), BF),
            ],
        ),
        out_shape=[jax.ShapeDtypeStruct((n, L, D), BF), jax.ShapeDtypeStruct((NR, 2, RANK, RB), F32)],
        compiler_params=params(1),
        name="attn_bwd",
    )(meta, q, k, v, p, o, dm, gf, u, w, sm, upb)


def after(value, other):
    return pl.pallas_call(
        lambda *refs: None,
        in_specs=[pl.BlockSpec(memory_space=pl.ANY)] * 2,
        out_specs=pl.BlockSpec(memory_space=pl.ANY),
        out_shape=jax.ShapeDtypeStruct(value.shape, value.dtype),
        input_output_aliases={0: 0},
        name="after",
    )(value, other)


def layer(meta, x, g, up, near, onward, rest):
    a, b = near
    upb, sm, vec, bi = small_params(meta, a, b, up)
    kept = ()
    for group in range(NR):
        last = group == NR - 1
        nxt = None if last else onward[0](a)
        out = attn_fwd(group, meta, x, a, b, upb, kept)
        kept, u = out[:-1], out[-1]
        if not last:
            a = after(nxt, u)
            b = onward[1](a, group)
    w, q, k, v, p, o, li = kept
    ho, gf, dm = ffn(meta, x, g, o, li, rest, vec, bi)
    hg, ag = attn_bwd(meta, q, k, v, p, o, dm, gf, u, w, sm, upb)
    return ho, hg, ag


def finish(ag, tokens):
    return ag.transpose(1, 2, 0, 3).reshape(2, RANK, D) * (2.0 / math.sqrt(tokens))


def meta_of(y, x, c, z, lens):
    rows = []
    for core in (c, 1 - c):
        for dy in range(2):
            for dx in range(2):
                rows.append((((y ^ dy) * 2 + (x ^ dx)) * 2 + core) * FB)
    head = jnp.stack([jnp.asarray(v, jnp.int32) for v in rows + [z] + [0] * 7])
    return jnp.concatenate([head, lens.reshape(-1)])


def device_plain(x, lens, qkv, wo, attn, down, up, gain, shift, wi, inb, wb, backb, g):
    tokens = x.shape[0] * L * lax.axis_size("fsdp") * lax.axis_size("rep")
    gather = lambda a, axis, dim: lax.all_gather(a, axis, axis=dim, tiled=True)
    both = lambda a, row, col: gather(gather(a, "rep", col), "fsdp", row)
    qkv, wo, wi, wb = both(qkv, 1, 2), both(wo, 0, 1), both(wi, 0, 1), both(wb, 0, 1)
    attn, down, gain, shift = (gather(a, "fsdp", 1) for a in (attn, down, gain, shift))
    inb, backb = gather(inb, "fsdp", 0), gather(backb, "fsdp", 0)

    def block(f, r):
        rows, cols = slice(FB * f, FB * f + FB), slice(RB * r, RB * r + RB)
        wide = slice(4 * FB * f, 4 * FB * f + 4 * FB)
        return pack(
            qkv[:, rows, cols], attn[:, rows], down[:, rows], gain[:, rows], shift[:, rows], inb[wide], backb[rows],
            wo[rows, cols], wi[rows, D * r : D * r + D], wb[wide, cols],
        )

    blocks = [[block(f, r) for r in range(NR)] for f in range(NF)]
    rest = jnp.stack([blocks[f][r][1] for f in range(NF) for r in range(NR)])
    firsts = [
        tuple(jnp.stack([blocks[2 * j + core][r][0] for j in range(4)]) for core in range(2)) for r in (0, 3, 2, 1)
    ]
    turn = iter(firsts[1:])
    ho, hg, ag = layer(
        meta_of(0, 0, 0, 0, lens), x, g, up, firsts[0],
        (lambda a: next(turn)[0], lambda a, group: firsts[group + 1][1]), rest,
    )
    return ho, hg, finish(lax.psum(ag, ("fsdp", "rep")), tokens)


AXES = ("y", "x", "c", "z")


def flip(value, dy=0, dx=0, dc=0, dz=0, shift=0):
    pairs = []
    for i in range(32):
        y, x, c, z = i >> 4, (i >> 3) & 1, (i >> 2) & 1, i & 3
        pairs.append((i, ((y ^ dy) << 4) | ((x ^ dx) << 3) | ((c ^ dc) << 2) | (((z ^ dz) + shift) & 3)))
    return lax.ppermute(value, AXES, pairs)


def device_block(x, lens, qkv, wo, attn, down, up, gain, shift, wi, inb, wb, backb, g):
    tokens = x.shape[0] * L * 32
    own, rest = pack(qkv, attn, down, gain, shift, inb, backb, wo, wi, wb)
    rest = lax.all_gather(rest, AXES, axis=0)
    meta = meta_of(lax.axis_index("y"), lax.axis_index("x"), lax.axis_index("c"), lax.axis_index("z"), lens)
    near = jnp.stack([own, flip(own, dx=1), flip(own, dy=1), flip(own, dy=1, dx=1)])
    onward = (lambda a: flip(a, shift=1), lambda a, group: flip(a, dc=1))
    ho, hg, ag = layer(meta, x, g, up, (near, flip(near, dc=1)), onward, rest)
    ag = ag + flip(ag, dc=1)
    ag = (ag + flip(ag, dx=1)) + (flip(ag, dy=1) + flip(ag, dy=1, dx=1))
    ag = (ag + flip(ag, dz=1)) + (flip(ag, dz=2) + flip(ag, dz=3))
    return ho, hg, finish(ag, tokens)


def solution(mesh):
    if mesh.shape["fsdp"] == NF and mesh.shape["rep"] == NR:
        mesh = Mesh(mesh.devices.reshape(2, 2, 2, 4), AXES)
        body, f, r = device_block, ("y", "x", "c"), ("z",)
    else:
        body, f, r = device_plain, ("fsdp",), ("rep",)
    items = P(f + r, None, None)
    in_specs = (
        items,
        P(f + r, None),
        P(None, f, r),
        P(f, r),
        P(None, f),
        P(None, f, None),
        P(),
        P(None, f),
        P(None, f),
        P(f, r),
        P(f),
        P(f, r),
        P(f),
        items,
    )

    def call(layer_input, lens, qkv, wo, attn, down, up, gain, shift, wi, inb, wb, backb, g):
        return jax.shard_map(
            body, mesh=mesh, in_specs=in_specs, out_specs=(items, items, P()), check_vma=False
        )(layer_input, lens, qkv, wo, attn, down, up, gain, shift, wi, inb, wb, backb, g)

    return call
```

```python
import math

import jax
import jax.numpy as jnp
from jax import lax
from jax.experimental import pallas as pl
from jax.experimental.pallas import tpu as pltpu
from jax.sharding import Mesh, PartitionSpec as P

D = 768
HD = 64
RANK = 8
L = 512
FF = 3072
F32 = jnp.float32
BF = jnp.bfloat16

NF = 8
NR = 4
FB = D // NF
RB = D // NR
GH = RB // HD
VMEM = 60 << 20

DOWN0 = 64
ATTN0 = 80
GAIN0 = 83
SHIFT0 = 85
INB0 = 87
BACKB0 = 91


def mm(a, b):
    return jnp.dot(a, b, preferred_element_type=F32)


def mm_nt(a, b):
    return lax.dot_general(a, b, (((1,), (1,)), ((), ())), preferred_element_type=F32)


def lanes(rows):
    return lax.broadcasted_iota(jnp.int32, (rows, 128), 1)


def params(n):
    return pltpu.CompilerParams(dimension_semantics=("arbitrary",) * n, vmem_limit_bytes=VMEM)


def whole_spec(*shape):
    return pl.BlockSpec(shape, lambda *_: (0,) * len(shape), pipeline_mode=pl.Buffered(1))


def pack_body(qkv_ref, attn_ref, down_ref, gain_ref, shift_ref, inb_ref, backb_ref, wo_ref, wi_ref, wb_ref,
              first_ref, rest_ref, scr):
    scr[...] = jnp.zeros_like(scr)
    up = lambda v: v.astype(F32)
    for k in range(2):
        scr[pl.ds(DOWN0 + RANK * k, RANK), :FB] = up(down_ref[k])
    inb = up(inb_ref[...])
    rows = [up(attn_ref[...]), up(gain_ref[...]), up(shift_ref[...])]
    rows += [inb[:, FB * j : FB * j + FB] for j in range(FF // D)] + [up(backb_ref[...])]
    at = ATTN0
    for v in rows:
        scr[pl.ds(at, v.shape[0]), :FB] = v
        at += v.shape[0]
    small = scr[...].T[:FB, 64:].astype(BF)
    for k in range(3):
        first_ref[k] = qkv_ref[k, :, :128]
    first_ref[3] = jnp.concatenate([qkv_ref[0, :, 128:], qkv_ref[1, :, 128:]], axis=1)
    first_ref[4] = jnp.concatenate([qkv_ref[2, :, 128:], small], axis=1)
    for j in range(6):
        rest_ref[j] = wi_ref[:, 128 * j : 128 * j + 128]
    rest_ref[6] = wo_ref[:, :128]
    rest_ref[7] = jnp.concatenate([wo_ref[:, 128:], wo_ref[:, 128:]], axis=1)
    for h in range(2):
        for j in range(3):
            rest_ref[8 + 3 * h + j] = wb_ref[FB * h : FB * h + FB, 128 * j : 128 * j + 128]


def pack(qkv, attn, down, gain, shift, inb, backb, wo, wi, wb):
    return pl.pallas_call(
        pack_body,
        out_shape=[jax.ShapeDtypeStruct((5, FB, 128), BF), jax.ShapeDtypeStruct((14, FB, 128), BF)],
        scratch_shapes=[pltpu.VMEM((128, 128), F32)],
        compiler_params=pltpu.CompilerParams(vmem_limit_bytes=VMEM),
        name="pack",
    )(qkv, attn, down.transpose(0, 2, 1), gain, shift, inb[None], backb[None], wo, wi, wb.T)


def small_body(meta, a_ref, b_ref, up_ref, upb_ref, sm_ref, vec_ref, inb_ref, scr):
    for j in range(4):
        scr[pl.ds(pl.multiple_of(meta[j], 32), FB), :] = a_ref[j, 0]
        scr[pl.ds(pl.multiple_of(meta[4 + j], 32), FB), :] = b_ref[j, 0]
    sm = scr[...]
    lane = lanes(D)
    sm_ref[...] = jnp.where(jnp.logical_and(lane >= DOWN0, lane < DOWN0 + 2 * RANK), sm, jnp.zeros((), BF))
    t = sm.astype(F32).T
    row = lambda i: t[i : i + 1]
    zero = jnp.zeros((1, D), F32)
    vec_ref[...] = jnp.concatenate(
        [row(ATTN0 + 2), row(GAIN0), row(SHIFT0), row(BACKB0), row(GAIN0 + 1), row(SHIFT0 + 1), zero, zero], axis=0
    )
    inb_ref[...] = jnp.concatenate(
        [t[INB0 + j : INB0 + j + 1, FB * f : FB * f + FB] for f in range(NF) for j in range(4)], axis=1
    )
    z = meta[8]
    zb = jnp.zeros((RANK, D), F32)
    for k in range(2):
        b = up_ref[k].astype(F32) * 2.0
        body = [jnp.zeros((DOWN0, D), F32)] + ([b, zb] if k == 0 else [zb, b])
        bias = jnp.broadcast_to(row(ATTN0 + k), (RANK, D))
        keep = lax.broadcasted_iota(jnp.int32, (RANK, D), 0) == 0
        body.append(jnp.where(keep, bias, 0.0))
        body.append(jnp.zeros((128 - DOWN0 - 3 * RANK, D), F32))
        full = jnp.concatenate(body, axis=0).astype(BF)
        for r in range(NR):
            part = full[:, RB * r : RB * r + RB]
            upb_ref[(z + NR - r) % NR, k] = jnp.concatenate([part, jnp.zeros((128, 256 - RB), BF)], axis=1)


def small_params(meta, a, b, up):
    tile = pl.BlockSpec((4, 1, FB, 128), lambda i, *_: (0, 4, 0, 0))
    return pl.pallas_call(
        small_body,
        grid_spec=pltpu.PrefetchScalarGridSpec(
            num_scalar_prefetch=1,
            grid=(1,),
            in_specs=[tile, tile, whole_spec(2, RANK, D)],
            out_specs=[whole_spec(NR, 2, 128, 256), whole_spec(D, 128), whole_spec(8, D), whole_spec(1, FF)],
            scratch_shapes=[pltpu.VMEM((D, 128), BF)],
        ),
        out_shape=[
            jax.ShapeDtypeStruct((NR, 2, 128, 256), BF),
            jax.ShapeDtypeStruct((D, 128), BF),
            jax.ShapeDtypeStruct((8, D), F32),
            jax.ShapeDtypeStruct((1, FF), F32),
        ],
        compiler_params=params(1),
        name="small_params",
    )(meta, a, b, up)


def attn_fwd_body(meta, x_ref, a_ref, b_ref, upb_ref, *refs):
    w_ref, q_ref, k_ref, v_ref, p_ref, o_ref, li_ref, u_ref = refs[-8:]
    i = pl.program_id(0)

    @pl.when(i == 0)
    def _():
        left = lanes(FB) < 64
        for src, base in ((a_ref, 0), (b_ref, 4)):
            for j in range(4):
                rows = pl.ds(pl.multiple_of(meta[base + j], 32), FB)
                for k in range(3):
                    w_ref[0, k, rows, :128] = src[j, k]
                t3 = src[j, 3]
                t4 = src[j, 4]
                w_ref[0, 0, rows, 128:] = jnp.where(left, t3, t4)
                w_ref[0, 1, rows, 128:] = jnp.concatenate([t3[:, 64:], t3[:, :64]], axis=1)
                w_ref[0, 2, rows, 128:] = t4

    x = x_ref[0]
    lane = lanes(L)
    raw = mm(x, w_ref[0, 0])
    u = raw[:, 128:].astype(BF)
    u = jnp.where(jnp.logical_and(lane >= DOWN0, lane < DOWN0 + 2 * RANK), u, jnp.zeros((), BF))
    u_ref[0] = u
    ua = jnp.where(lane == ATTN0, jnp.ones((), BF), u)
    q = (raw + mm(ua, upb_ref[0, 0])).astype(BF) * jnp.asarray(0.125, BF)
    k = mm(x, w_ref[0, 1]).astype(BF)
    v = (mm(x, w_ref[0, 2]) + mm(ua, upb_ref[0, 1])).astype(BF)
    live = meta[16 + 2 * i] + meta[17 + 2 * i]
    mask = jnp.where(lax.broadcasted_iota(jnp.int32, (1, L), 1) < live, 0.0, -1e30)
    left = lane < HD
    zero = jnp.zeros((), BF)
    one = jnp.ones((), BF)
    for t in range(2):
        c = slice(128 * t, 128 * t + 128)
        qp, kp, vp = q[:, c], k[:, c], v[:, c]
        q_ref[0, 0, t] = qp
        k_ref[0, 0, t] = kp
        v_ref[0, 0, t] = vp
        acc = None
        for h in range(2 * t, min(2 * t + 2, GH)):
            own = left if h % 2 == 0 else jnp.logical_not(left)
            s = mm_nt(qp, jnp.where(own, kp, zero)) + mask
            m = jnp.max(s, axis=1, keepdims=True)
            pb = jnp.exp(s - m).astype(BF)
            p_ref[0, 0, h] = pb
            rhs = jnp.concatenate([jnp.where(own, vp, zero), jnp.where(own, one, zero)], axis=1)
            part = mm(pb, rhs)
            acc = part if acc is None else acc + part
        total = acc[:, 128:]
        if 2 * t + 1 >= GH:
            total = jnp.where(left, total, 1.0)
        li = 1.0 / total
        li_ref[0, 0, t] = li
        o_ref[0, 0, t] = (acc[:, :128] * li).astype(BF)


def attn_fwd(group, meta, x, a, b, upb, kept):
    n = x.shape[0]
    shapes = [
        ((NR, 3, D, 256), BF),
        ((NR, n, 2, L, 128), BF),
        ((NR, n, 2, L, 128), BF),
        ((NR, n, 2, L, 128), BF),
        ((NR, n, GH, L, L), BF),
        ((NR, n, 2, L, 128), BF),
        ((NR, n, 2, L, 128), F32),
    ]
    specs = [pl.BlockSpec((1, 3, D, 256), lambda i, *_: (group, 0, 0, 0), pipeline_mode=pl.Buffered(1))]
    specs += [pl.BlockSpec((1, 1) + s[2:], lambda i, *_: (group, i, 0, 0, 0)) for s, _ in shapes[1:]]
    specs.append(pl.BlockSpec((1, L, 128), lambda i, *_: (i, 0, 0)))
    out_shape = [jax.ShapeDtypeStruct(s, d) for s, d in shapes] + [jax.ShapeDtypeStruct((n, L, 128), BF)]
    return pl.pallas_call(
        attn_fwd_body,
        grid_spec=pltpu.PrefetchScalarGridSpec(
            num_scalar_prefetch=1,
            grid=(n,),
            in_specs=[
                pl.BlockSpec((1, L, D), lambda i, *_: (i, 0, 0)),
                whole_spec(4, 5, FB, 128),
                whole_spec(4, 5, FB, 128),
                pl.BlockSpec((1, 2, 128, 256), lambda i, *_: (group, 0, 0, 0), pipeline_mode=pl.Buffered(1)),
            ]
            + [pl.BlockSpec(memory_space=pl.ANY)] * len(kept),
            out_specs=specs,
        ),
        out_shape=out_shape,
        input_output_aliases={5 + j: j for j in range(len(kept))},
        compiler_params=params(1),
        name="attn_fwd",
    )(meta, x, a, b, upb, *kept)


def bf(v):
    return jnp.asarray(v, BF)


def gelu_pair(z):
    cdf = 0.5 + 0.5 * lax.erf(z * math.sqrt(0.5))
    zb = z.astype(BF)
    pdf = jnp.exp2(zb * zb * bf(-0.5 * math.log2(math.e))) * bf(1.0 / math.sqrt(2.0 * math.pi))
    return (z * cdf).astype(BF), cdf.astype(BF) + zb * pdf


def ln_stats(v):
    c = v - jnp.mean(v, axis=-1, keepdims=True)
    r = lax.rsqrt(jnp.mean(c * c, axis=-1, keepdims=True) + 1e-5)
    return c * r, r


def ln_back(g, n, r, w):
    c = g * w
    return r * (c - jnp.mean(c, axis=-1, keepdims=True) - n * jnp.mean(c * n, axis=-1, keepdims=True))


TT = 256
FC = 512


def ffn_body(meta, x_ref, g_ref, o_ref, li_ref, r_ref, vec_ref, bi_ref, ho_ref, gf_ref, dm_ref,
             wo_scr, wi_scr, wb_scr, act_scr, dact_scr, gi_scr):
    @pl.when(jnp.logical_and(pl.program_id(0) == 0, pl.program_id(1) == 0))
    def _():
        z = meta[8]

        def block(f, carry):
            rows = pl.ds(pl.multiple_of(f * FB, 32), FB)
            tile = lambda r, j: r_ref[NR * f + r, j]
            left = lambda r, j: r_ref[NR * f + r, j, :, :64]
            for r in range(NR):
                for j in range(6):
                    wi_scr[rows, pl.ds(D * r + 128 * j, 128)] = tile(r, j)
            slot = ((z + NR - f // 2) % NR) * 2 + f % 2
            wo_scr[pl.ds(pl.multiple_of(slot * FB, 32), FB), :] = jnp.concatenate(
                sum([[tile(r, 6), left(r, 7)] for r in range(NR)], []), axis=1
            )
            for r in range(NR):
                for h in range(2):
                    for j in range(3):
                        cols = pl.ds(pl.multiple_of(f * 4 * FB + 128 * j, 128), 128)
                        wb_scr[RB * r + FB * h : RB * r + FB * h + FB, cols] = tile(r, 8 + 3 * h + j)
            return carry

        lax.fori_loop(0, NF, block, 0)

    x = x_ref[0].astype(F32)
    mixed = jnp.concatenate(sum([[o_ref[g, 0, 0], o_ref[g, 0, 1][:, :64]] for g in range(NR)], []), axis=1)
    n1, r1 = ln_stats(x + mm(mixed, wo_scr[...]) + vec_ref[0:1])
    h1 = n1 * vec_ref[1:2] + vec_ref[2:3]
    h1b = h1.astype(BF)
    for c in range(FF // FC):
        s = pl.ds(c * FC, FC)
        a, d = gelu_pair(mm(h1b, wi_scr[:, s]) + bi_ref[0:1, s])
        act_scr[:, s] = a
        dact_scr[:, s] = d
    n2, r2 = ln_stats(h1 + mm_nt(act_scr[...], wb_scr[...]) + vec_ref[3:4])
    ho_ref[0] = (n2 * vec_ref[4:5] + vec_ref[5:6]).astype(BF)
    gs = ln_back(g_ref[0].astype(F32), n2, r2, vec_ref[4:5])
    gsb = gs.astype(BF)
    for c in range(FF // FC):
        s = pl.ds(c * FC, FC)
        ga = mm(gsb, wb_scr[:, s])
        gi_scr[:, s] = ga.astype(BF) * dact_scr[:, s]
    gh = gs + mm_nt(gi_scr[...], wi_scr[...])
    gf = ln_back(gh, n1, r1, vec_ref[1:2])
    gf_ref[0] = gf
    gm = mm_nt(gf.astype(BF), wo_scr[...])
    for g in range(NR):
        part = gm[:, RB * g : RB * g + RB]
        dm_ref[g, 0, 0] = (part[:, :128] * li_ref[g, 0, 0]).astype(BF)
        tail = part[:, 128:] * li_ref[g, 0, 1][:, :64]
        dm_ref[g, 0, 1] = jnp.concatenate([tail, jnp.zeros((TT, 64), F32)], axis=1).astype(BF)


def ffn(meta, x, g, o, li, rest, vec, bi):
    n = x.shape[0]
    row = pl.BlockSpec((1, TT, D), lambda i, t, *_: (i, t, 0))
    prow = pl.BlockSpec((NR, 1, 2, TT, 128), lambda i, t, *_: (0, i, 0, t, 0))
    return pl.pallas_call(
        ffn_body,
        grid_spec=pltpu.PrefetchScalarGridSpec(
            num_scalar_prefetch=1,
            grid=(n, L // TT),
            in_specs=[row, row, prow, prow, whole_spec(NF * NR, 14, FB, 128), whole_spec(8, D), whole_spec(1, FF)],
            out_specs=[row, row, prow],
            scratch_shapes=[pltpu.VMEM((D, D), BF), pltpu.VMEM((D, FF), BF), pltpu.VMEM((D, FF), BF)]
            + [pltpu.VMEM((TT, FF), BF)] * 3,
        ),
        out_shape=[
            jax.ShapeDtypeStruct((n, L, D), BF),
            jax.ShapeDtypeStruct((n, L, D), F32),
            jax.ShapeDtypeStruct((NR, n, 2, L, 128), BF),
        ],
        compiler_params=params(2),
        name="ffn",
    )(meta, x, g, o, li, rest, vec, bi)


def attn_bwd_body(meta, q_ref, k_ref, v_ref, p_ref, o_ref, dm_ref, gf_ref, u_ref, w_ref, sm_ref, upb_ref,
                  hg_ref, ag_ref, w_scr, up_scr, acc_scr, dq_scr, dkt_scr, dvt_scr):
    i = pl.program_id(0)
    cat = lambda parts: jnp.concatenate(parts, axis=1)

    @pl.when(i == 0)
    def _():
        for k in range(3):
            w_scr[k] = cat([w_ref[g, k][:, :RB] for g in range(NR)])
        for k in range(2):
            up_scr[k] = cat([upb_ref[g, k][:, :RB] for g in range(NR)])
        acc_scr[...] = jnp.zeros_like(acc_scr)

    def group(g, carry):
        left = lanes(L) < HD
        zero = jnp.zeros((), BF)
        neg = jnp.asarray(-1.0, BF)
        for t in range(2):
            qp, kp, vp = q_ref[g, 0, t], k_ref[g, 0, t], v_ref[g, 0, t]
            dm = dm_ref[g, 0, t]
            lhs = jnp.concatenate([dm, dm * o_ref[g, 0, t]], axis=1)
            qt = qp.T
            dmt = dm.T
            dq = None
            for h in range(2 * t, min(2 * t + 2, GH)):
                own = left if h % 2 == 0 else jnp.logical_not(left)
                rhs = jnp.concatenate([jnp.where(own, vp, zero), jnp.where(own, neg, zero)], axis=1)
                p = p_ref[g, 0, h]
                ds = (p.astype(F32) * mm_nt(lhs, rhs)).astype(BF)
                part = mm(ds, jnp.where(own, kp, zero))
                dq = part if dq is None else dq + part
                src = slice(HD * (h % 2), HD * (h % 2) + HD)
                dst = slice(HD * h, HD * h + HD)
                dkt_scr[g, dst, :] = mm(qt[src, :], ds).astype(BF)
                dvt_scr[g, dst, :] = mm(dmt[src, :], p).astype(BF)
            dq_scr[g, t] = (dq * 0.125).astype(BF)
        return carry

    lax.fori_loop(0, NR, group, 0)
    dq = cat(sum([[dq_scr[g, 0], dq_scr[g, 1][:, :64]] for g in range(NR)], []))
    dk = cat([dkt_scr[g].T for g in range(NR)])
    dv = cat([dvt_scr[g].T for g in range(NR)])
    gu = (mm_nt(dq, up_scr[0]) + mm_nt(dv, up_scr[1])).astype(BF)
    hg = gf_ref[0] + mm_nt(dq, w_scr[0]) + mm_nt(dk, w_scr[1]) + mm_nt(dv, w_scr[2]) + mm_nt(gu, sm_ref[...])
    hg_ref[0] = hg.astype(BF)
    ut = u_ref[0].T
    acc_scr[0] += mm(ut[DOWN0 : DOWN0 + RANK], dq)
    acc_scr[1] += mm(ut[DOWN0 + RANK : DOWN0 + 2 * RANK], dv)

    @pl.when(i == pl.num_programs(0) - 1)
    def _():
        for g in range(NR):
            ag_ref[(meta[8] + NR - g) % NR] = acc_scr[:, :, RB * g : RB * g + RB]


def attn_bwd(meta, q, k, v, p, o, dm, gf, u, w, sm, upb):
    n = gf.shape[0]
    tile = pl.BlockSpec((NR, 1, 2, L, 128), lambda i, *_: (0, i, 0, 0, 0))
    return pl.pallas_call(
        attn_bwd_body,
        grid_spec=pltpu.PrefetchScalarGridSpec(
            num_scalar_prefetch=1,
            grid=(n,),
            in_specs=[tile] * 3
            + [pl.BlockSpec((NR, 1, GH, L, L), lambda i, *_: (0, i, 0, 0, 0))]
            + [tile] * 2
            + [
                pl.BlockSpec((1, L, D), lambda i, *_: (i, 0, 0)),
                pl.BlockSpec((1, L, 128), lambda i, *_: (i, 0, 0)),
                whole_spec(NR, 3, D, 256),
                whole_spec(D, 128),
                whole_spec(NR, 2, 128, 256),
            ],
            out_specs=[pl.BlockSpec((1, L, D), lambda i, *_: (i, 0, 0)), whole_spec(NR, 2, RANK, RB)],
            scratch_shapes=[
                pltpu.VMEM((3, D, D), BF),
                pltpu.VMEM((2, 128, D), BF),
                pltpu.VMEM((2, RANK, D), F32),
                pltpu.VMEM((NR, 2, L, 128), BF),
                pltpu.VMEM((NR, RB, L), BF),
                pltpu.VMEM((NR, RB, L), BF),
            ],
        ),
        out_shape=[jax.ShapeDtypeStruct((n, L, D), BF), jax.ShapeDtypeStruct((NR, 2, RANK, RB), F32)],
        compiler_params=params(1),
        name="attn_bwd",
    )(meta, q, k, v, p, o, dm, gf, u, w, sm, upb)


def after(value, other):
    return pl.pallas_call(
        lambda *refs: None,
        in_specs=[pl.BlockSpec(memory_space=pl.ANY)] * 2,
        out_specs=pl.BlockSpec(memory_space=pl.ANY),
        out_shape=jax.ShapeDtypeStruct(value.shape, value.dtype),
        input_output_aliases={0: 0},
        name="after",
    )(value, other)


def layer(meta, x, g, up, near, onward, rest):
    a, b = near
    upb, sm, vec, bi = small_params(meta, a, b, up)
    kept = ()
    for group in range(NR):
        last = group == NR - 1
        nxt = None if last else onward[0](a)
        out = attn_fwd(group, meta, x, a, b, upb, kept)
        kept, u = out[:-1], out[-1]
        if not last:
            a = after(nxt, u)
            b = onward[1](a, group)
    w, q, k, v, p, o, li = kept
    ho, gf, dm = ffn(meta, x, g, o, li, rest, vec, bi)
    hg, ag = attn_bwd(meta, q, k, v, p, o, dm, gf, u, w, sm, upb)
    return ho, hg, ag


def finish(ag, tokens):
    return ag.transpose(1, 2, 0, 3).reshape(2, RANK, D) * (2.0 / math.sqrt(tokens))


def meta_of(y, x, c, z, lens):
    rows = []
    for core in (c, 1 - c):
        for dy in range(2):
            for dx in range(2):
                rows.append((((y ^ dy) * 2 + (x ^ dx)) * 2 + core) * FB)
    head = jnp.stack([jnp.asarray(v, jnp.int32) for v in rows + [z] + [0] * 7])
    return jnp.concatenate([head, lens.reshape(-1)])


def device_plain(x, lens, qkv, wo, attn, down, up, gain, shift, wi, inb, wb, backb, g):
    tokens = x.shape[0] * L * lax.axis_size("fsdp") * lax.axis_size("rep")
    gather = lambda a, axis, dim: lax.all_gather(a, axis, axis=dim, tiled=True)
    both = lambda a, row, col: gather(gather(a, "rep", col), "fsdp", row)
    qkv, wo, wi, wb = both(qkv, 1, 2), both(wo, 0, 1), both(wi, 0, 1), both(wb, 0, 1)
    attn, down, gain, shift = (gather(a, "fsdp", 1) for a in (attn, down, gain, shift))
    inb, backb = gather(inb, "fsdp", 0), gather(backb, "fsdp", 0)

    def block(f, r):
        rows, cols = slice(FB * f, FB * f + FB), slice(RB * r, RB * r + RB)
        wide = slice(4 * FB * f, 4 * FB * f + 4 * FB)
        return pack(
            qkv[:, rows, cols], attn[:, rows], down[:, rows], gain[:, rows], shift[:, rows], inb[wide], backb[rows],
            wo[rows, cols], wi[rows, D * r : D * r + D], wb[wide, cols],
        )

    blocks = [[block(f, r) for r in range(NR)] for f in range(NF)]
    rest = jnp.stack([blocks[f][r][1] for f in range(NF) for r in range(NR)])
    firsts = [
        tuple(jnp.stack([blocks[2 * j + core][r][0] for j in range(4)]) for core in range(2)) for r in (0, 3, 2, 1)
    ]
    turn = iter(firsts[1:])
    ho, hg, ag = layer(
        meta_of(0, 0, 0, 0, lens), x, g, up, firsts[0],
        (lambda a: next(turn)[0], lambda a, group: firsts[group + 1][1]), rest,
    )
    return ho, hg, finish(lax.psum(ag, ("fsdp", "rep")), tokens)


AXES = ("y", "x", "c", "z")


def flip(value, dy=0, dx=0, dc=0, dz=0, shift=0):
    pairs = []
    for i in range(32):
        y, x, c, z = i >> 4, (i >> 3) & 1, (i >> 2) & 1, i & 3
        pairs.append((i, ((y ^ dy) << 4) | ((x ^ dx) << 3) | ((c ^ dc) << 2) | (((z ^ dz) + shift) & 3)))
    return lax.ppermute(value, AXES, pairs)


def device_block(x, lens, qkv, wo, attn, down, up, gain, shift, wi, inb, wb, backb, g):
    tokens = x.shape[0] * L * 32
    own, rest = pack(qkv, attn, down, gain, shift, inb, backb, wo, wi, wb)
    rest = lax.all_gather(rest, AXES, axis=0)
    meta = meta_of(lax.axis_index("y"), lax.axis_index("x"), lax.axis_index("c"), lax.axis_index("z"), lens)
    near = jnp.stack([own, flip(own, dx=1), flip(own, dy=1), flip(own, dy=1, dx=1)])
    onward = (lambda a: flip(a, shift=1), lambda a, group: flip(a, dc=1))
    ho, hg, ag = layer(meta, x, g, up, (near, flip(near, dc=1)), onward, rest)
    ag = ag + flip(ag, dc=1)
    ag = (ag + flip(ag, dx=1)) + (flip(ag, dy=1) + flip(ag, dy=1, dx=1))
    ag = (ag + flip(ag, dz=1)) + (flip(ag, dz=2) + flip(ag, dz=3))
    return ho, hg, finish(ag, tokens)


def solution(mesh):
    if mesh.shape["fsdp"] == NF and mesh.shape["rep"] == NR:
        mesh = Mesh(mesh.devices.reshape(2, 2, 2, 4), AXES)
        body, f, r = device_block, ("y", "x", "c"), ("z",)
    else:
        body, f, r = device_plain, ("fsdp",), ("rep",)
    items = P(f + r, None, None)
    in_specs = (
        items,
        P(f + r, None),
        P(None, f, r),
        P(f, r),
        P(None, f),
        P(None, f, None),
        P(),
        P(None, f),
        P(None, f),
        P(f, r),
        P(f),
        P(f, r),
        P(f),
        items,
    )

    def call(layer_input, lens, qkv, wo, attn, down, up, gain, shift, wi, inb, wb, backb, g):
        return jax.shard_map(
            body, mesh=mesh, in_specs=in_specs, out_specs=(items, items, P()), check_vma=False
        )(layer_input, lens, qkv, wo, attn, down, up, gain, shift, wi, inb, wb, backb, g)

    return call
```

```python
import math

import jax
import jax.numpy as jnp
from jax import lax
from jax.experimental import pallas as pl
from jax.experimental.pallas import tpu as pltpu
from jax.sharding import Mesh, PartitionSpec as P

D = 768
HD = 64
RANK = 8
L = 512
FF = 3072
F32 = jnp.float32
BF = jnp.bfloat16

NF = 8
NR = 4
FB = D // NF
RB = D // NR
NP = D // 128
NH = 2 * NP
STEPS = 2
SP = NP // STEPS
SW = 128 * SP
VMEM = 60 << 20

DOWN0 = 64
ATTN0 = 80
GAIN0 = 83
SHIFT0 = 85
INB0 = 87
BACKB0 = 91


def mm(a, b):
    return jnp.dot(a, b, preferred_element_type=F32)


def mm_nt(a, b):
    return lax.dot_general(a, b, (((1,), (1,)), ((), ())), preferred_element_type=F32)


def lanes(rows):
    return lax.broadcasted_iota(jnp.int32, (rows, 128), 1)


def params(n):
    return pltpu.CompilerParams(dimension_semantics=("arbitrary",) * n, vmem_limit_bytes=VMEM)


def whole_spec(*shape):
    return pl.BlockSpec(shape, lambda *_: (0,) * len(shape), pipeline_mode=pl.Buffered(1))


def pack_body(qkv_ref, attn_ref, down_ref, gain_ref, shift_ref, inb_ref, backb_ref, wo_ref, wi_ref, wb_ref,
              first_ref, rest_ref, again_ref, scr):
    scr[...] = jnp.zeros_like(scr)
    up = lambda v: v.astype(F32)
    for k in range(2):
        scr[pl.ds(DOWN0 + RANK * k, RANK), :FB] = up(down_ref[k])
    inb = up(inb_ref[...])
    rows = [up(attn_ref[...]), up(gain_ref[...]), up(shift_ref[...])]
    rows += [inb[:, FB * j : FB * j + FB] for j in range(FF // D)] + [up(backb_ref[...])]
    at = ATTN0
    for v in rows:
        scr[pl.ds(at, v.shape[0]), :FB] = v
        at += v.shape[0]
    small = scr[...].T[:FB, 64:].astype(BF)
    for k in range(3):
        first_ref[k] = qkv_ref[k, :, :128]
    first_ref[3] = jnp.concatenate([qkv_ref[0, :, 128:], qkv_ref[1, :, 128:]], axis=1)
    first_ref[4] = jnp.concatenate([qkv_ref[2, :, 128:], small], axis=1)
    for j in range(6):
        rest_ref[j] = wi_ref[:, 128 * j : 128 * j + 128]
    rest_ref[6] = wo_ref[:, :128]
    rest_ref[7] = jnp.concatenate([wo_ref[:, 128:], wo_ref[:, 128:]], axis=1)
    for h in range(2):
        for j in range(3):
            rest_ref[8 + 3 * h + j] = wb_ref[FB * h : FB * h + FB, 128 * j : 128 * j + 128]
    again_ref[...] = rest_ref[...]


def pack(qkv, attn, down, gain, shift, inb, backb, wo, wi, wb):
    return pl.pallas_call(
        pack_body,
        out_shape=[jax.ShapeDtypeStruct((5, FB, 128), BF), jax.ShapeDtypeStruct((14, FB, 128), BF),
                   jax.ShapeDtypeStruct((14, FB, 128), BF)],
        scratch_shapes=[pltpu.VMEM((128, 128), F32)],
        compiler_params=pltpu.CompilerParams(vmem_limit_bytes=VMEM),
        name="pack",
    )(qkv, attn, down.transpose(0, 2, 1), gain, shift, inb[None], backb[None], wo, wi, wb.T)


def assemble(meta, src, up_ref, w_ref, sm_ref, upb_ref, vec_ref, bi_ref, scr):
    z = meta[8]
    for s in range(NF):
        rows = pl.ds(pl.multiple_of(meta[s], 32), FB)
        parts = [[], [], []]
        for r in range(NR):
            slot = z ^ r
            t3, t4 = src[s][slot, 3], src[s][slot, 4]
            parts[0] += [src[s][slot, 0], t3[:, :64]]
            parts[1] += [src[s][slot, 1], t3[:, 64:]]
            parts[2] += [src[s][slot, 2], t4[:, :64]]
        for k in range(3):
            w_ref[k, rows, :] = jnp.concatenate(parts[k], axis=1)
        scr[rows, :] = src[s][0, 4]
    sm = scr[...]
    lane = lanes(D)
    sm_ref[...] = jnp.where(jnp.logical_and(lane >= DOWN0, lane < DOWN0 + 2 * RANK), sm, jnp.zeros((), BF))
    t = sm.astype(F32).T
    row = lambda i: t[i : i + 1]
    zero = jnp.zeros((1, D), F32)
    vec_ref[...] = jnp.concatenate(
        [row(ATTN0 + 2), row(GAIN0), row(SHIFT0), row(BACKB0), row(GAIN0 + 1), row(SHIFT0 + 1), zero, zero], axis=0
    )
    bi_ref[...] = jnp.concatenate(
        [t[INB0 + j : INB0 + j + 1, FB * f : FB * f + FB] for f in range(NF) for j in range(4)], axis=1
    )
    zb = jnp.zeros((RANK, D), F32)
    for k in range(2):
        b = up_ref[k].astype(F32) * 2.0
        body = [jnp.zeros((DOWN0, D), F32)] + ([b, zb] if k == 0 else [zb, b])
        bias = jnp.broadcast_to(row(ATTN0 + k), (RANK, D))
        keep = lax.broadcasted_iota(jnp.int32, (RANK, D), 0) == 0
        body.append(jnp.where(keep, bias, 0.0))
        body.append(jnp.zeros((128 - DOWN0 - 3 * RANK, D), F32))
        upb_ref[k] = jnp.concatenate(body, axis=0).astype(BF)


def attn_fwd_body(meta, x_ref, up_ref, *refs):
    src = refs[:NF]
    w_ref, sm_ref, upb_ref, vec_ref, bi_ref, q_ref, k_ref, v_ref, p_ref, o_ref, li_ref, u_ref, scr = refs[NF:]
    i, step = pl.program_id(0), pl.program_id(1)

    @pl.when(jnp.logical_and(i == 0, step == 0))
    def _():
        assemble(meta, src, up_ref, w_ref, sm_ref, upb_ref, vec_ref, bi_ref, scr)

    lane = lanes(L)

    @pl.when(step == 0)
    def _():
        x = x_ref[0]
        u = mm(x, sm_ref[...]).astype(BF)
        u_ref[0] = u
        ua = jnp.where(lane == ATTN0, jnp.ones((), BF), u)
        for c in range(D // 256):
            s = slice(256 * c, 256 * c + 256)
            q = mm(x, w_ref[0, :, s]) + mm(ua, upb_ref[0, :, s])
            q_ref[0, :, s] = q.astype(BF) * jnp.asarray(0.125, BF)
            k_ref[0, :, s] = mm(x, w_ref[1, :, s]).astype(BF)
            v_ref[0, :, s] = (mm(x, w_ref[2, :, s]) + mm(ua, upb_ref[1, :, s])).astype(BF)

    live = meta[16 + 2 * i] + meta[17 + 2 * i]
    mask = jnp.where(lax.broadcasted_iota(jnp.int32, (1, L), 1) < live, 0.0, -1e30)
    left = lane < HD
    zero = jnp.zeros((), BF)
    one = jnp.ones((), BF)
    for j in range(SP):
        tile = pl.ds(pl.multiple_of(step * SW + 128 * j, 128), 128)
        qp, kp, vp = q_ref[0, :, tile], k_ref[0, :, tile], v_ref[0, :, tile]
        acc = None
        for h in range(2):
            own = left if h == 0 else jnp.logical_not(left)
            s = mm_nt(qp, jnp.where(own, kp, zero)) + mask
            m = jnp.max(s, axis=1, keepdims=True)
            pb = jnp.exp(s - m).astype(BF)
            p_ref[0, 2 * j + h] = pb
            rhs = jnp.concatenate([jnp.where(own, vp, zero), jnp.where(own, one, zero)], axis=1)
            part = mm(pb, rhs)
            acc = part if acc is None else acc + part
        li = 1.0 / acc[:, 128:]
        c = slice(128 * j, 128 * j + 128)
        li_ref[0, :, c] = li
        o_ref[0, :, c] = (acc[:, :128] * li).astype(BF)


def item_spec(*shape):
    return pl.BlockSpec((1,) + shape, lambda i, *_: (i,) + (0,) * len(shape))


def step_spec():
    return pl.BlockSpec((1, L, SW), lambda i, t, *_: (i, 0, t))


def probs_spec():
    return pl.BlockSpec((1, 2 * SP, L, L), lambda i, t, *_: (i, t, 0, 0))


def attn_fwd(meta, x, up, firsts):
    n = x.shape[0]
    wide = lambda d: jax.ShapeDtypeStruct((n, L, D), d)
    consts = [((3, D, D), BF), ((D, 128), BF), ((2, 128, D), BF), ((8, D), F32), ((1, FF), F32)]
    return pl.pallas_call(
        attn_fwd_body,
        grid_spec=pltpu.PrefetchScalarGridSpec(
            num_scalar_prefetch=1,
            grid=(n, STEPS),
            in_specs=[item_spec(L, D), whole_spec(2, RANK, D)] + [whole_spec(NR, 5, FB, 128)] * NF,
            out_specs=[whole_spec(*s) for s, _ in consts]
            + [item_spec(L, D)] * 3
            + [probs_spec(), step_spec(), step_spec(), item_spec(L, 128)],
            scratch_shapes=[pltpu.VMEM((D, 128), BF)],
        ),
        out_shape=[jax.ShapeDtypeStruct(s, d) for s, d in consts]
        + [wide(BF)] * 3
        + [jax.ShapeDtypeStruct((n, NH, L, L), BF), wide(BF), wide(F32), jax.ShapeDtypeStruct((n, L, 128), BF)],
        compiler_params=params(2),
        name="attn_fwd",
    )(meta, x, up, *firsts)


def bf(v):
    return jnp.asarray(v, BF)


def gelu_pair(z):
    cdf = 0.5 + 0.5 * lax.erf(z * math.sqrt(0.5))
    zb = z.astype(BF)
    pdf = jnp.exp2(zb * zb * bf(-0.5 * math.log2(math.e))) * bf(1.0 / math.sqrt(2.0 * math.pi))
    return (z * cdf).astype(BF), cdf.astype(BF) + zb * pdf


def ln_stats(v):
    c = v - jnp.mean(v, axis=-1, keepdims=True)
    r = lax.rsqrt(jnp.mean(c * c, axis=-1, keepdims=True) + 1e-5)
    return c * r, r


def ln_back(g, n, r, w):
    c = g * w
    return r * (c - jnp.mean(c, axis=-1, keepdims=True) - n * jnp.mean(c * n, axis=-1, keepdims=True))


TT = 256
FC = 512


def ffn_body(meta, x_ref, g_ref, o_ref, li_ref, vec_ref, bi_ref, *refs):
    near, far = refs[:NF], refs[NF : 2 * NF]
    ho_ref, gf_ref, dm_ref, wo_scr, wi_scr, wb_scr, act_scr, dact_scr, gi_scr = refs[2 * NF :]

    @pl.when(jnp.logical_and(pl.program_id(0) == 0, pl.program_id(1) == 0))
    def _():
        z = meta[8]
        for s in range(NF):
            rows = pl.ds(pl.multiple_of(meta[s], 32), FB)
            for k in range(NR):
                tile = lambda i: near[s][i] if k == 0 else far[s][k - 1, i]
                r = z ^ k
                for i in range(6):
                    wi_scr[rows, pl.ds(pl.multiple_of(r * D + 128 * i, 128), 128)] = tile(i)
                for h in range(2):
                    down = pl.ds(pl.multiple_of(r * RB + FB * h, 32), FB)
                    for i in range(3):
                        cols = pl.ds(pl.multiple_of(meta[s] * 4 + 128 * i, 128), 128)
                        wb_scr[down, cols] = tile(8 + 3 * h + i)
            blocks = []
            for r in range(NR):
                slot = z ^ r
                for i, width in ((6, 128), (7, 64)):
                    blocks.append(jnp.where(slot == 0, near[s][i], far[s][jnp.maximum(slot - 1, 0), i])[:, :width])
            wo_scr[rows, :] = jnp.concatenate(blocks, axis=1)

    x = x_ref[0].astype(F32)
    n1, r1 = ln_stats(x + mm(o_ref[0], wo_scr[...]) + vec_ref[0:1])
    h1 = n1 * vec_ref[1:2] + vec_ref[2:3]
    h1b = h1.astype(BF)
    for c in range(FF // FC):
        s = pl.ds(c * FC, FC)
        a, d = gelu_pair(mm(h1b, wi_scr[:, s]) + bi_ref[0:1, s])
        act_scr[:, s] = a
        dact_scr[:, s] = d
    n2, r2 = ln_stats(h1 + mm_nt(act_scr[...], wb_scr[...]) + vec_ref[3:4])
    ho_ref[0] = (n2 * vec_ref[4:5] + vec_ref[5:6]).astype(BF)
    gs = ln_back(g_ref[0].astype(F32), n2, r2, vec_ref[4:5])
    gsb = gs.astype(BF)
    for c in range(FF // FC):
        s = pl.ds(c * FC, FC)
        ga = mm(gsb, wb_scr[:, s])
        gi_scr[:, s] = ga.astype(BF) * dact_scr[:, s]
    gh = gs + mm_nt(gi_scr[...], wi_scr[...])
    gf = ln_back(gh, n1, r1, vec_ref[1:2])
    gf_ref[0] = gf
    gm = mm_nt(gf.astype(BF), wo_scr[...])
    dm_ref[0] = (gm * li_ref[0]).astype(BF)


def ffn(meta, x, g, o, li, vec, bi, near, far):
    n = x.shape[0]
    row = pl.BlockSpec((1, TT, D), lambda i, t, *_: (i, t, 0))
    return pl.pallas_call(
        ffn_body,
        grid_spec=pltpu.PrefetchScalarGridSpec(
            num_scalar_prefetch=1,
            grid=(n, L // TT),
            in_specs=[row] * 4
            + [whole_spec(8, D), whole_spec(1, FF)]
            + [whole_spec(14, FB, 128)] * NF
            + [whole_spec(NR - 1, 14, FB, 128)] * NF,
            out_specs=[row] * 3,
            scratch_shapes=[pltpu.VMEM((D, D), BF), pltpu.VMEM((D, FF), BF), pltpu.VMEM((D, FF), BF)]
            + [pltpu.VMEM((TT, FF), BF)] * 3,
        ),
        out_shape=[jax.ShapeDtypeStruct((n, L, D), d) for d in (BF, F32, BF)],
        compiler_params=params(2),
        name="ffn",
    )(meta, x, g, o, li, vec, bi, *near, *far)


def attn_bwd_body(meta, q_ref, k_ref, v_ref, p_ref, o_ref, dm_ref, gf_ref, u_ref, w_ref, sm_ref, upb_ref,
                  hg_ref, ag_ref, dq_scr, dkt_scr, dvt_scr):
    i, step = pl.program_id(0), pl.program_id(1)

    @pl.when(jnp.logical_and(i == 0, step == 0))
    def _():
        ag_ref[...] = jnp.zeros_like(ag_ref)

    left = lanes(L) < HD
    zero = jnp.zeros((), BF)
    neg = jnp.asarray(-1.0, BF)
    for j in range(SP):
        c = slice(128 * j, 128 * j + 128)
        at = step * SW + 128 * j
        kp, vp, dm = k_ref[0, :, c], v_ref[0, :, c], dm_ref[0, :, c]
        lhs = jnp.concatenate([dm, dm * o_ref[0, :, c]], axis=1)
        qt = q_ref[0, :, c].T
        dmt = dm.T
        dq = None
        for h in range(2):
            own = left if h == 0 else jnp.logical_not(left)
            rhs = jnp.concatenate([jnp.where(own, vp, zero), jnp.where(own, neg, zero)], axis=1)
            p = p_ref[0, 2 * j + h]
            ds = (p.astype(F32) * mm_nt(lhs, rhs)).astype(BF)
            part = mm(ds, jnp.where(own, kp, zero))
            dq = part if dq is None else dq + part
            src = slice(HD * h, HD * h + HD)
            dst = pl.ds(pl.multiple_of(at + HD * h, HD), HD)
            dkt_scr[dst, :] = mm(qt[src, :], ds).astype(BF)
            dvt_scr[dst, :] = mm(dmt[src, :], p).astype(BF)
        dq_scr[:, pl.ds(pl.multiple_of(at, 128), 128)] = (dq * 0.125).astype(BF)

    @pl.when(step == STEPS - 1)
    def _():
        dq = dq_scr[...]
        dk = dkt_scr[...].T
        dv = dvt_scr[...].T
        gu = (mm_nt(dq, upb_ref[0]) + mm_nt(dv, upb_ref[1])).astype(BF)
        hg = gf_ref[0] + mm_nt(dq, w_ref[0]) + mm_nt(dk, w_ref[1]) + mm_nt(dv, w_ref[2]) + mm_nt(gu, sm_ref[...])
        hg_ref[0] = hg.astype(BF)
        ut = u_ref[0].T
        ag_ref[0] += mm(ut[DOWN0 : DOWN0 + RANK], dq)
        ag_ref[1] += mm(ut[DOWN0 + RANK : DOWN0 + 2 * RANK], dv)


def attn_bwd(meta, q, k, v, p, o, dm, gf, u, w, sm, upb):
    n = gf.shape[0]
    return pl.pallas_call(
        attn_bwd_body,
        grid_spec=pltpu.PrefetchScalarGridSpec(
            num_scalar_prefetch=1,
            grid=(n, STEPS),
            in_specs=[step_spec()] * 3
            + [probs_spec()]
            + [step_spec()] * 2
            + [item_spec(L, D), item_spec(L, 128), whole_spec(3, D, D), whole_spec(D, 128), whole_spec(2, 128, D)],
            out_specs=[item_spec(L, D), whole_spec(2, RANK, D)],
            scratch_shapes=[pltpu.VMEM((L, D), BF), pltpu.VMEM((D, L), BF), pltpu.VMEM((D, L), BF)],
        ),
        out_shape=[jax.ShapeDtypeStruct((n, L, D), BF), jax.ShapeDtypeStruct((2, RANK, D), F32)],
        compiler_params=params(2),
        name="attn_bwd",
    )(meta, q, k, v, p, o, dm, gf, u, w, sm, upb)


def after(value, *others):
    return pl.pallas_call(
        lambda *refs: None,
        in_specs=[pl.BlockSpec(memory_space=pl.ANY)] * (1 + len(others)),
        out_specs=pl.BlockSpec(memory_space=pl.ANY),
        out_shape=jax.ShapeDtypeStruct(value.shape, value.dtype),
        input_output_aliases={0: 0},
        name="after",
    )(value, *others)


def layer(meta, x, g, up, firsts, near, far):
    w, sm, upb, vec, bi, q, k, v, p, o, li, u = attn_fwd(meta, x, up, firsts)
    ho, gf, dm = ffn(meta, x, g, o, li, vec, bi, near, far(u))
    hg, ag = attn_bwd(meta, q, k, v, p, o, dm, gf, u, w, sm, upb)
    return ho, hg, ag


def finish(ag, tokens):
    return ag * (2.0 / math.sqrt(tokens))


def meta_of(y, x, c, z, lens):
    rows = []
    for core in (c, 1 - c):
        for dy in range(2):
            for dx in range(2):
                rows.append((((y ^ dy) * 2 + (x ^ dx)) * 2 + core) * FB)
    head = jnp.stack([jnp.asarray(v, jnp.int32) for v in rows + [z] + [0] * 7])
    return jnp.concatenate([head, lens.reshape(-1)])


def device_plain(x, lens, qkv, wo, attn, down, up, gain, shift, wi, inb, wb, backb, g):
    tokens = x.shape[0] * L * lax.axis_size("fsdp") * lax.axis_size("rep")
    gather = lambda a, axis, dim: lax.all_gather(a, axis, axis=dim, tiled=True)
    both = lambda a, row, col: gather(gather(a, "rep", col), "fsdp", row)
    qkv, wo, wi, wb = both(qkv, 1, 2), both(wo, 0, 1), both(wi, 0, 1), both(wb, 0, 1)
    attn, down, gain, shift = (gather(a, "fsdp", 1) for a in (attn, down, gain, shift))
    inb, backb = gather(inb, "fsdp", 0), gather(backb, "fsdp", 0)

    def block(f, r):
        rows, cols = slice(FB * f, FB * f + FB), slice(RB * r, RB * r + RB)
        wide = slice(4 * FB * f, 4 * FB * f + 4 * FB)
        return pack(
            qkv[:, rows, cols], attn[:, rows], down[:, rows], gain[:, rows], shift[:, rows], inb[wide], backb[rows],
            wo[rows, cols], wi[rows, D * r : D * r + D], wb[wide, cols],
        )

    blocks = [[block(f, r) for r in range(NR)] for f in range(NF)]
    order = [2 * j + core for core in range(2) for j in range(NF // 2)]
    firsts = [jnp.stack([blocks[f][r][0] for r in range(NR)]) for f in order]
    near = [blocks[f][0][1] for f in order]
    far = [jnp.stack([blocks[f][r][1] for r in range(1, NR)]) for f in order]
    ho, hg, ag = layer(meta_of(0, 0, 0, 0, lens), x, g, up, firsts, near, lambda u: far)
    return ho, hg, finish(lax.psum(ag, ("fsdp", "rep")), tokens)


AXES = ("y", "x", "c", "z")


def flip(value, dy=0, dx=0, dc=0, dz=0):
    pairs = []
    for i in range(32):
        y, x, c, z = i >> 4, (i >> 3) & 1, (i >> 2) & 1, i & 3
        pairs.append((i, ((y ^ dy) << 4) | ((x ^ dx) << 3) | ((c ^ dc) << 2) | (z ^ dz)))
    return lax.ppermute(value, AXES, pairs)


def along_z(value):
    return [flip(value, dz=k) for k in range(1, NR)]


def across(value):
    return [flip(value, dx=1), flip(value, dy=1), flip(value, dy=1, dx=1)]


def both_cores(values):
    return values + [flip(v, dc=1) for v in values]


def device_block(x, lens, qkv, wo, attn, down, up, gain, shift, wi, inb, wb, backb, g):
    tokens = x.shape[0] * L * 32
    own, rest, rest_again = pack(qkv, attn, down, gain, shift, inb, backb, wo, wi, wb)
    line = jnp.stack([own] + along_z(own))
    sides = across(rest)
    rest_line = jnp.stack(along_z(after(rest_again, line)))
    near = both_cores([rest] + sides)
    first_sides = across(after(line, *sides))
    firsts = both_cores([line] + first_sides)
    rest_line = after(rest_line, *first_sides)
    rest_far = across(rest_line)

    def far(u):
        return both_cores([rest_line] + [after(v, u) for v in rest_far])

    meta = meta_of(lax.axis_index("y"), lax.axis_index("x"), lax.axis_index("c"), lax.axis_index("z"), lens)
    meta = after(meta, rest_line, *near)
    ho, hg, ag = layer(meta, x, g, up, firsts, near, far)
    ag = ag + flip(ag, dc=1)
    a, b, c = across(ag)
    ag = (ag + a) + (b + c)
    a, b, c = along_z(ag)
    ag = (ag + a) + (b + c)
    return ho, hg, finish(ag, tokens)


def solution(mesh):
    if mesh.shape["fsdp"] == NF and mesh.shape["rep"] == NR:
        mesh = Mesh(mesh.devices.reshape(2, 2, 2, 4), AXES)
        body, f, r = device_block, ("y", "x", "c"), ("z",)
    else:
        body, f, r = device_plain, ("fsdp",), ("rep",)
    items = P(f + r, None, None)
    in_specs = (
        items,
        P(f + r, None),
        P(None, f, r),
        P(f, r),
        P(None, f),
        P(None, f, None),
        P(),
        P(None, f),
        P(None, f),
        P(f, r),
        P(f),
        P(f, r),
        P(f),
        items,
    )

    def call(layer_input, lens, qkv, wo, attn, down, up, gain, shift, wi, inb, wb, backb, g):
        return jax.shard_map(
            body, mesh=mesh, in_specs=in_specs, out_specs=(items, items, P()), check_vma=False
        )(layer_input, lens, qkv, wo, attn, down, up, gain, shift, wi, inb, wb, backb, g)

    return call
```

```python
import math

import jax
import jax.numpy as jnp
from jax import lax
from jax.experimental import pallas as pl
from jax.experimental.pallas import tpu as pltpu
from jax.sharding import Mesh, PartitionSpec as P

D = 768
HD = 64
RANK = 8
L = 512
FF = 3072
F32 = jnp.float32
BF = jnp.bfloat16

NF = 8
NR = 4
FB = D // NF
RB = D // NR
NP = D // 128
NH = 2 * NP
STEPS = 2
SP = NP // STEPS
SW = 128 * SP
VMEM = 60 << 20

DOWN0 = 64
ATTN0 = 80
GAIN0 = 83
SHIFT0 = 85
INB0 = 87
BACKB0 = 91


def mm(a, b):
    return jnp.dot(a, b, preferred_element_type=F32)


def mm_nt(a, b):
    return lax.dot_general(a, b, (((1,), (1,)), ((), ())), preferred_element_type=F32)


def lanes(rows):
    return lax.broadcasted_iota(jnp.int32, (rows, 128), 1)


def params(n):
    return pltpu.CompilerParams(dimension_semantics=("arbitrary",) * n, vmem_limit_bytes=VMEM)


def whole_spec(*shape):
    return pl.BlockSpec(shape, lambda *_: (0,) * len(shape), pipeline_mode=pl.Buffered(1))


def pack_body(qkv_ref, attn_ref, down_ref, gain_ref, shift_ref, inb_ref, backb_ref, wo_ref, wi_ref, wb_ref,
              first_ref, rest_ref, again_ref, scr):
    scr[...] = jnp.zeros_like(scr)
    up = lambda v: v.astype(F32)
    for k in range(2):
        scr[pl.ds(DOWN0 + RANK * k, RANK), :FB] = up(down_ref[k])
    inb = up(inb_ref[...])
    rows = [up(attn_ref[...]), up(gain_ref[...]), up(shift_ref[...])]
    rows += [inb[:, FB * j : FB * j + FB] for j in range(FF // D)] + [up(backb_ref[...])]
    at = ATTN0
    for v in rows:
        scr[pl.ds(at, v.shape[0]), :FB] = v
        at += v.shape[0]
    small = scr[...].T[:FB, 64:].astype(BF)
    for k in range(3):
        first_ref[k] = qkv_ref[k, :, :128]
    first_ref[3] = jnp.concatenate([qkv_ref[0, :, 128:], qkv_ref[1, :, 128:]], axis=1)
    first_ref[4] = jnp.concatenate([qkv_ref[2, :, 128:], small], axis=1)
    for j in range(6):
        rest_ref[j] = wi_ref[:, 128 * j : 128 * j + 128]
    rest_ref[6] = wo_ref[:, :128]
    rest_ref[7] = jnp.concatenate([wo_ref[:, 128:], wo_ref[:, 128:]], axis=1)
    for h in range(2):
        for j in range(3):
            rest_ref[8 + 3 * h + j] = wb_ref[FB * h : FB * h + FB, 128 * j : 128 * j + 128]
    again_ref[...] = rest_ref[...]


def pack(qkv, attn, down, gain, shift, inb, backb, wo, wi, wb):
    return pl.pallas_call(
        pack_body,
        out_shape=[jax.ShapeDtypeStruct((5, FB, 128), BF), jax.ShapeDtypeStruct((14, FB, 128), BF),
                   jax.ShapeDtypeStruct((14, FB, 128), BF)],
        scratch_shapes=[pltpu.VMEM((128, 128), F32)],
        compiler_params=pltpu.CompilerParams(vmem_limit_bytes=VMEM),
        name="pack",
    )(qkv, attn, down.transpose(0, 2, 1), gain, shift, inb[None], backb[None], wo, wi, wb.T)


def assemble(meta, src, up_ref, w_ref, sm_ref, upb_ref, vec_ref, bi_ref, scr):
    z = meta[8]
    for s in range(NF):
        rows = pl.ds(pl.multiple_of(meta[s], 32), FB)
        parts = [[], [], []]
        for r in range(NR):
            slot = z ^ r
            t3, t4 = src[s][slot, 3], src[s][slot, 4]
            parts[0] += [src[s][slot, 0], t3[:, :64]]
            parts[1] += [src[s][slot, 1], t3[:, 64:]]
            parts[2] += [src[s][slot, 2], t4[:, :64]]
        for k in range(3):
            w_ref[k, rows, :] = jnp.concatenate(parts[k], axis=1)
        scr[rows, :] = src[s][0, 4]
    sm = scr[...]
    lane = lanes(D)
    sm_ref[...] = jnp.where(jnp.logical_and(lane >= DOWN0, lane < DOWN0 + 2 * RANK), sm, jnp.zeros((), BF))
    t = sm.astype(F32).T
    row = lambda i: t[i : i + 1]
    zero = jnp.zeros((1, D), F32)
    vec_ref[...] = jnp.concatenate(
        [row(ATTN0 + 2), row(GAIN0), row(SHIFT0), row(BACKB0), row(GAIN0 + 1), row(SHIFT0 + 1), zero, zero], axis=0
    )
    bi_ref[...] = jnp.concatenate(
        [t[INB0 + j : INB0 + j + 1, FB * f : FB * f + FB] for f in range(NF) for j in range(4)], axis=1
    )
    zb = jnp.zeros((RANK, D), F32)
    for k in range(2):
        b = up_ref[k].astype(F32) * 2.0
        body = [jnp.zeros((DOWN0, D), F32)] + ([b, zb] if k == 0 else [zb, b])
        bias = jnp.broadcast_to(row(ATTN0 + k), (RANK, D))
        keep = lax.broadcasted_iota(jnp.int32, (RANK, D), 0) == 0
        body.append(jnp.where(keep, bias, 0.0))
        body.append(jnp.zeros((128 - DOWN0 - 3 * RANK, D), F32))
        upb_ref[k] = jnp.concatenate(body, axis=0).astype(BF)


def attn_fwd_body(meta, x_ref, up_ref, *refs):
    src = refs[:NF]
    w_ref, sm_ref, upb_ref, vec_ref, bi_ref, q_ref, k_ref, v_ref, p_ref, o_ref, li_ref, u_ref, scr = refs[NF:]
    i, step = pl.program_id(0), pl.program_id(1)

    @pl.when(jnp.logical_and(i == 0, step == 0))
    def _():
        assemble(meta, src, up_ref, w_ref, sm_ref, upb_ref, vec_ref, bi_ref, scr)

    lane = lanes(L)

    @pl.when(step == 0)
    def _():
        x = x_ref[0]
        u = mm(x, sm_ref[...]).astype(BF)
        u_ref[0] = u
        ua = jnp.where(lane == ATTN0, jnp.ones((), BF), u)
        for c in range(D // 256):
            s = slice(256 * c, 256 * c + 256)
            q = mm(x, w_ref[0, :, s]) + mm(ua, upb_ref[0, :, s])
            q_ref[0, :, s] = q.astype(BF) * jnp.asarray(0.125, BF)
            k_ref[0, :, s] = mm(x, w_ref[1, :, s]).astype(BF)
            v_ref[0, :, s] = (mm(x, w_ref[2, :, s]) + mm(ua, upb_ref[1, :, s])).astype(BF)

    live = meta[16 + 2 * i] + meta[17 + 2 * i]
    mask = jnp.where(lax.broadcasted_iota(jnp.int32, (1, L), 1) < live, 0.0, -1e30)
    left = lane < HD
    zero = jnp.zeros((), BF)
    one = jnp.ones((), BF)
    for j in range(SP):
        tile = pl.ds(pl.multiple_of(step * SW + 128 * j, 128), 128)
        qp, kp, vp = q_ref[0, :, tile], k_ref[0, :, tile], v_ref[0, :, tile]
        acc = None
        for h in range(2):
            own = left if h == 0 else jnp.logical_not(left)
            s = mm_nt(qp, jnp.where(own, kp, zero)) + mask
            m = jnp.max(s, axis=1, keepdims=True)
            pb = jnp.exp(s - m).astype(BF)
            p_ref[0, 2 * j + h] = pb
            rhs = jnp.concatenate([jnp.where(own, vp, zero), jnp.where(own, one, zero)], axis=1)
            part = mm(pb, rhs)
            acc = part if acc is None else acc + part
        li = 1.0 / acc[:, 128:]
        c = slice(128 * j, 128 * j + 128)
        li_ref[0, :, c] = li
        o_ref[0, :, c] = (acc[:, :128] * li).astype(BF)


def item_spec(*shape):
    return pl.BlockSpec((1,) + shape, lambda i, *_: (i,) + (0,) * len(shape))


def step_spec():
    return pl.BlockSpec((1, L, SW), lambda i, t, *_: (i, 0, t))


def probs_spec():
    return pl.BlockSpec((1, 2 * SP, L, L), lambda i, t, *_: (i, t, 0, 0))


def attn_fwd(meta, x, up, firsts):
    n = x.shape[0]
    wide = lambda d: jax.ShapeDtypeStruct((n, L, D), d)
    consts = [((3, D, D), BF), ((D, 128), BF), ((2, 128, D), BF), ((8, D), F32), ((1, FF), F32)]
    return pl.pallas_call(
        attn_fwd_body,
        grid_spec=pltpu.PrefetchScalarGridSpec(
            num_scalar_prefetch=1,
            grid=(n, STEPS),
            in_specs=[item_spec(L, D), whole_spec(2, RANK, D)] + [whole_spec(NR, 5, FB, 128)] * NF,
            out_specs=[whole_spec(*s) for s, _ in consts]
            + [item_spec(L, D)] * 3
            + [probs_spec(), step_spec(), step_spec(), item_spec(L, 128)],
            scratch_shapes=[pltpu.VMEM((D, 128), BF)],
        ),
        out_shape=[jax.ShapeDtypeStruct(s, d) for s, d in consts]
        + [wide(BF)] * 3
        + [jax.ShapeDtypeStruct((n, NH, L, L), BF), wide(BF), wide(F32), jax.ShapeDtypeStruct((n, L, 128), BF)],
        compiler_params=params(2),
        name="attn_fwd",
    )(meta, x, up, *firsts)


def bf(v):
    return jnp.asarray(v, BF)


def gelu_pair(z):
    cdf = 0.5 + 0.5 * lax.erf(z * math.sqrt(0.5))
    zb = z.astype(BF)
    pdf = jnp.exp2(zb * zb * bf(-0.5 * math.log2(math.e))) * bf(1.0 / math.sqrt(2.0 * math.pi))
    return (z * cdf).astype(BF), cdf.astype(BF) + zb * pdf


def ln_stats(v):
    c = v - jnp.mean(v, axis=-1, keepdims=True)
    r = lax.rsqrt(jnp.mean(c * c, axis=-1, keepdims=True) + 1e-5)
    return c * r, r


def ln_back(g, n, r, w):
    c = g * w
    return r * (c - jnp.mean(c, axis=-1, keepdims=True) - n * jnp.mean(c * n, axis=-1, keepdims=True))


TT = 512
FC = 512


def ffn_body(meta, x_ref, g_ref, o_ref, li_ref, vec_ref, bi_ref, *refs):
    near, far = refs[:NF], refs[NF : 2 * NF]
    ho_ref, gf_ref, dm_ref, wo_scr, wi_scr, wb_scr, act_scr, dact_scr, gi_scr = refs[2 * NF :]

    @pl.when(jnp.logical_and(pl.program_id(0) == 0, pl.program_id(1) == 0))
    def _():
        z = meta[8]
        for s in range(NF):
            rows = pl.ds(pl.multiple_of(meta[s], 32), FB)
            for k in range(NR):
                tile = lambda i: near[s][i] if k == 0 else far[s][k - 1, i]
                r = z ^ k
                for i in range(6):
                    wi_scr[rows, pl.ds(pl.multiple_of(r * D + 128 * i, 128), 128)] = tile(i)
                for h in range(2):
                    down = pl.ds(pl.multiple_of(r * RB + FB * h, 32), FB)
                    for i in range(3):
                        cols = pl.ds(pl.multiple_of(meta[s] * 4 + 128 * i, 128), 128)
                        wb_scr[down, cols] = tile(8 + 3 * h + i)
            blocks = []
            for r in range(NR):
                slot = z ^ r
                for i, width in ((6, 128), (7, 64)):
                    blocks.append(jnp.where(slot == 0, near[s][i], far[s][jnp.maximum(slot - 1, 0), i])[:, :width])
            wo_scr[rows, :] = jnp.concatenate(blocks, axis=1)

    x = x_ref[0].astype(F32)
    n1, r1 = ln_stats(x + mm(o_ref[0], wo_scr[...]) + vec_ref[0:1])
    h1 = n1 * vec_ref[1:2] + vec_ref[2:3]
    h1b = h1.astype(BF)
    for c in range(FF // FC):
        s = pl.ds(c * FC, FC)
        a, d = gelu_pair(mm(h1b, wi_scr[:, s]) + bi_ref[0:1, s])
        act_scr[:, s] = a
        dact_scr[:, s] = d
    n2, r2 = ln_stats(h1 + mm_nt(act_scr[...], wb_scr[...]) + vec_ref[3:4])
    ho_ref[0] = (n2 * vec_ref[4:5] + vec_ref[5:6]).astype(BF)
    gs = ln_back(g_ref[0].astype(F32), n2, r2, vec_ref[4:5])
    gsb = gs.astype(BF)
    for c in range(FF // FC):
        s = pl.ds(c * FC, FC)
        ga = mm(gsb, wb_scr[:, s])
        gi_scr[:, s] = ga.astype(BF) * dact_scr[:, s]
    gh = gs + mm_nt(gi_scr[...], wi_scr[...])
    gf = ln_back(gh, n1, r1, vec_ref[1:2])
    gf_ref[0] = gf
    gm = mm_nt(gf.astype(BF), wo_scr[...])
    dm_ref[0] = (gm * li_ref[0]).astype(BF)


def ffn(meta, x, g, o, li, vec, bi, near, far):
    n = x.shape[0]
    row = pl.BlockSpec((1, TT, D), lambda i, t, *_: (i, t, 0))
    return pl.pallas_call(
        ffn_body,
        grid_spec=pltpu.PrefetchScalarGridSpec(
            num_scalar_prefetch=1,
            grid=(n, L // TT),
            in_specs=[row] * 4
            + [whole_spec(8, D), whole_spec(1, FF)]
            + [whole_spec(14, FB, 128)] * NF
            + [whole_spec(NR - 1, 14, FB, 128)] * NF,
            out_specs=[row] * 3,
            scratch_shapes=[pltpu.VMEM((D, D), BF), pltpu.VMEM((D, FF), BF), pltpu.VMEM((D, FF), BF)]
            + [pltpu.VMEM((TT, FF), BF)] * 3,
        ),
        out_shape=[jax.ShapeDtypeStruct((n, L, D), d) for d in (BF, F32, BF)],
        compiler_params=params(2),
        name="ffn",
    )(meta, x, g, o, li, vec, bi, *near, *far)


def attn_bwd_body(meta, q_ref, k_ref, v_ref, p_ref, o_ref, dm_ref, gf_ref, u_ref, w_ref, sm_ref, upb_ref,
                  hg_ref, ag_ref, dq_scr, dkt_scr, dvt_scr):
    i, step = pl.program_id(0), pl.program_id(1)

    @pl.when(jnp.logical_and(i == 0, step == 0))
    def _():
        ag_ref[...] = jnp.zeros_like(ag_ref)

    left = lanes(L) < HD
    zero = jnp.zeros((), BF)
    neg = jnp.asarray(-1.0, BF)
    for j in range(SP):
        c = slice(128 * j, 128 * j + 128)
        at = step * SW + 128 * j
        kp, vp, dm = k_ref[0, :, c], v_ref[0, :, c], dm_ref[0, :, c]
        lhs = jnp.concatenate([dm, dm * o_ref[0, :, c]], axis=1)
        qt = q_ref[0, :, c].T
        dmt = dm.T
        dq = None
        for h in range(2):
            own = left if h == 0 else jnp.logical_not(left)
            rhs = jnp.concatenate([jnp.where(own, vp, zero), jnp.where(own, neg, zero)], axis=1)
            p = p_ref[0, 2 * j + h]
            ds = (p.astype(F32) * mm_nt(lhs, rhs)).astype(BF)
            part = mm(ds, jnp.where(own, kp, zero))
            dq = part if dq is None else dq + part
            src = slice(HD * h, HD * h + HD)
            dst = pl.ds(pl.multiple_of(at + HD * h, HD), HD)
            dkt_scr[dst, :] = mm(qt[src, :], ds).astype(BF)
            dvt_scr[dst, :] = mm(dmt[src, :], p).astype(BF)
        dq_scr[:, pl.ds(pl.multiple_of(at, 128), 128)] = (dq * 0.125).astype(BF)

    @pl.when(step == STEPS - 1)
    def _():
        dq = dq_scr[...]
        dk = dkt_scr[...].T
        dv = dvt_scr[...].T
        gu = (mm_nt(dq, upb_ref[0]) + mm_nt(dv, upb_ref[1])).astype(BF)
        hg = gf_ref[0] + mm_nt(dq, w_ref[0]) + mm_nt(dk, w_ref[1]) + mm_nt(dv, w_ref[2]) + mm_nt(gu, sm_ref[...])
        hg_ref[0] = hg.astype(BF)
        ut = u_ref[0].T
        ag_ref[0] += mm(ut[DOWN0 : DOWN0 + RANK], dq)
        ag_ref[1] += mm(ut[DOWN0 + RANK : DOWN0 + 2 * RANK], dv)


def attn_bwd(meta, q, k, v, p, o, dm, gf, u, w, sm, upb):
    n = gf.shape[0]
    return pl.pallas_call(
        attn_bwd_body,
        grid_spec=pltpu.PrefetchScalarGridSpec(
            num_scalar_prefetch=1,
            grid=(n, STEPS),
            in_specs=[step_spec()] * 3
            + [probs_spec()]
            + [step_spec()] * 2
            + [item_spec(L, D), item_spec(L, 128), whole_spec(3, D, D), whole_spec(D, 128), whole_spec(2, 128, D)],
            out_specs=[item_spec(L, D), whole_spec(2, RANK, D)],
            scratch_shapes=[pltpu.VMEM((L, D), BF), pltpu.VMEM((D, L), BF), pltpu.VMEM((D, L), BF)],
        ),
        out_shape=[jax.ShapeDtypeStruct((n, L, D), BF), jax.ShapeDtypeStruct((2, RANK, D), F32)],
        compiler_params=params(2),
        name="attn_bwd",
    )(meta, q, k, v, p, o, dm, gf, u, w, sm, upb)


def after(value, *others):
    return pl.pallas_call(
        lambda *refs: None,
        in_specs=[pl.BlockSpec(memory_space=pl.ANY)] * (1 + len(others)),
        out_specs=pl.BlockSpec(memory_space=pl.ANY),
        out_shape=jax.ShapeDtypeStruct(value.shape, value.dtype),
        input_output_aliases={0: 0},
        name="after",
    )(value, *others)


def layer(meta, x, g, up, firsts, near, far):
    w, sm, upb, vec, bi, q, k, v, p, o, li, u = attn_fwd(meta, x, up, firsts)
    ho, gf, dm = ffn(meta, x, g, o, li, vec, bi, near, far(u))
    hg, ag = attn_bwd(meta, q, k, v, p, o, dm, gf, u, w, sm, upb)
    return ho, hg, ag


def finish(ag, tokens):
    return ag * (2.0 / math.sqrt(tokens))


def meta_of(y, x, c, z, lens):
    rows = []
    for core in (c, 1 - c):
        for dy in range(2):
            for dx in range(2):
                rows.append((((y ^ dy) * 2 + (x ^ dx)) * 2 + core) * FB)
    head = jnp.stack([jnp.asarray(v, jnp.int32) for v in rows + [z] + [0] * 7])
    return jnp.concatenate([head, lens.reshape(-1)])


def device_plain(x, lens, qkv, wo, attn, down, up, gain, shift, wi, inb, wb, backb, g):
    tokens = x.shape[0] * L * lax.axis_size("fsdp") * lax.axis_size("rep")
    gather = lambda a, axis, dim: lax.all_gather(a, axis, axis=dim, tiled=True)
    both = lambda a, row, col: gather(gather(a, "rep", col), "fsdp", row)
    qkv, wo, wi, wb = both(qkv, 1, 2), both(wo, 0, 1), both(wi, 0, 1), both(wb, 0, 1)
    attn, down, gain, shift = (gather(a, "fsdp", 1) for a in (attn, down, gain, shift))
    inb, backb = gather(inb, "fsdp", 0), gather(backb, "fsdp", 0)

    def block(f, r):
        rows, cols = slice(FB * f, FB * f + FB), slice(RB * r, RB * r + RB)
        wide = slice(4 * FB * f, 4 * FB * f + 4 * FB)
        return pack(
            qkv[:, rows, cols], attn[:, rows], down[:, rows], gain[:, rows], shift[:, rows], inb[wide], backb[rows],
            wo[rows, cols], wi[rows, D * r : D * r + D], wb[wide, cols],
        )

    blocks = [[block(f, r) for r in range(NR)] for f in range(NF)]
    order = [2 * j + core for core in range(2) for j in range(NF // 2)]
    firsts = [jnp.stack([blocks[f][r][0] for r in range(NR)]) for f in order]
    near = [blocks[f][0][1] for f in order]
    far = [jnp.stack([blocks[f][r][1] for r in range(1, NR)]) for f in order]
    ho, hg, ag = layer(meta_of(0, 0, 0, 0, lens), x, g, up, firsts, near, lambda u: far)
    return ho, hg, finish(lax.psum(ag, ("fsdp", "rep")), tokens)


AXES = ("y", "x", "c", "z")


def flip(value, dy=0, dx=0, dc=0, dz=0):
    pairs = []
    for i in range(32):
        y, x, c, z = i >> 4, (i >> 3) & 1, (i >> 2) & 1, i & 3
        pairs.append((i, ((y ^ dy) << 4) | ((x ^ dx) << 3) | ((c ^ dc) << 2) | (z ^ dz)))
    return lax.ppermute(value, AXES, pairs)


def along_z(value):
    return [flip(value, dz=k) for k in range(1, NR)]


def across(value):
    return [flip(value, dx=1), flip(value, dy=1), flip(value, dy=1, dx=1)]


def both_cores(values):
    return values + [flip(v, dc=1) for v in values]


def device_block(x, lens, qkv, wo, attn, down, up, gain, shift, wi, inb, wb, backb, g):
    tokens = x.shape[0] * L * 32
    own, rest, rest_again = pack(qkv, attn, down, gain, shift, inb, backb, wo, wi, wb)
    line = jnp.stack([own] + along_z(own))
    sides = across(rest)
    rest_again = after(rest_again, line)
    rest_line = jnp.stack(along_z(rest_again))
    near = both_cores([rest] + sides)
    line = after(line, rest_again, *sides)
    first_sides = across(line)
    firsts = both_cores([line] + first_sides)
    rest_line = after(rest_line, *first_sides)
    rest_far = across(rest_line)

    def far(u):
        return both_cores([rest_line] + [after(v, u) for v in rest_far])

    meta = meta_of(lax.axis_index("y"), lax.axis_index("x"), lax.axis_index("c"), lax.axis_index("z"), lens)
    meta = after(meta, rest_line, *near)
    ho, hg, ag = layer(meta, x, g, up, firsts, near, far)
    ag = ag + flip(ag, dc=1)
    a, b, c = across(ag)
    ag = (ag + a) + (b + c)
    a, b, c = along_z(ag)
    ag = (ag + a) + (b + c)
    return ho, hg, finish(ag, tokens)


def solution(mesh):
    if mesh.shape["fsdp"] == NF and mesh.shape["rep"] == NR:
        mesh = Mesh(mesh.devices.reshape(2, 2, 2, 4), AXES)
        body, f, r = device_block, ("y", "x", "c"), ("z",)
    else:
        body, f, r = device_plain, ("fsdp",), ("rep",)
    items = P(f + r, None, None)
    in_specs = (
        items,
        P(f + r, None),
        P(None, f, r),
        P(f, r),
        P(None, f),
        P(None, f, None),
        P(),
        P(None, f),
        P(None, f),
        P(f, r),
        P(f),
        P(f, r),
        P(f),
        items,
    )

    def call(layer_input, lens, qkv, wo, attn, down, up, gain, shift, wi, inb, wb, backb, g):
        return jax.shard_map(
            body, mesh=mesh, in_specs=in_specs, out_specs=(items, items, P()), check_vma=False
        )(layer_input, lens, qkv, wo, attn, down, up, gain, shift, wi, inb, wb, backb, g)

    return call
```
